128 devices in a mesh: tm: 32 (over x, z, core), panel: 4 (over y).
Axes of the slice: x: 4, y: 4, z: 4, core: 2. Of those that a mesh axis runs over, the one named last changes fastest.
Arguments:
- design: bfloat16 [8192, 7680], P('tm', 'panel'), may hold values from -6 to 6
- partials: bfloat16 [8192, 64], P('tm'), may hold values from -0.119628906 to 0.119628906
- observed: bfloat16 [8192], P('tm'), may hold values from -6 to 6
- arc_of_row: int32 [8192, 1], replicated, may hold values from 0 to 31, as said below
- autoreg: float32 [32], replicated, may hold values from -0.55 to 0.5
- movavg: float32 [32], replicated, may hold values from 0.3 to 0.9
Outputs:
- normal: float32 [7680, 7680], P('tm', 'panel')
- right_hand: float32 [7680], P('panel')
The draws below stay inside these ranges and needn't reach their ends.
Inputs may be any that keep to these rules, and one draw needn't show every extreme that they name: arc_of_row never falls along the epochs and names every arc; arcs 2b and 2b + 1 together have 2 * 256 epochs, one of them 384 // 3 to 160 epochs and the other 352 to 384; one arc has exactly 384 epochs and its partner exactly 128, so that at most 12 rows of one device belong to one arc, and every device holds exactly 12 rows of the longest arc; arc a is held by index a of tm.
All inputs are finite; a program needn't handle non-finite values.
Results may differ from the reference program's by a relative error of at most 0.02.
Values may be sent and summed in bfloat16 or wider, within the bound.
A program may use at most 192 MiB of HBM per device.

```python
import jax
import jax.numpy as jnp
from jax import lax

NC = 7680
NA = 64
ROW_DEV = 256
ROWS = 8192
ARCS = 32
SLOTS = 384
N_TM = 32


def draw_arc_of_row(key, part):
    half_rows = ROW_DEV // 2
    least_shift = 3 * half_rows // 4
    pair_count = ARCS // 2
    key_shift = jax.random.fold_in(key, 11)
    key_pick = jax.random.fold_in(key, 12)
    key_sign = jax.random.fold_in(key, 13)
    key_signs = jax.random.fold_in(key, 14)
    magnitude = jax.random.randint(key_shift, (pair_count,), least_shift, half_rows + 1)
    signs = jax.random.randint(key_signs, (pair_count,), 0, 2) * 2 - 1
    shifts = magnitude * signs
    chosen = jax.random.randint(key_pick, (), 0, pair_count)
    sign_value = jax.random.randint(key_sign, (), 0, 2) * 2 - 1
    shifts = jnp.where(jnp.arange(pair_count) == chosen, sign_value * half_rows, shifts)
    lengths = jnp.stack([ROW_DEV + shifts, ROW_DEV - shifts], axis=1).reshape(ARCS)
    ends = jnp.cumsum(lengths)
    epochs = jnp.arange(ROWS, dtype=jnp.int32)
    arcs = jnp.sum((epochs[:, None] >= ends[None, :]).astype(jnp.int32), axis=1)
    return arcs.astype(jnp.int32).reshape(ROWS, 1)


def noise_coefficients(key):
    key_ar = jax.random.fold_in(key, 21)
    key_ma = jax.random.fold_in(key, 22)
    ma_values = jax.random.uniform(key_ma, (ARCS,), jnp.float32, 0.3, 0.9)
    ar_values = jax.random.uniform(key_ar, (ARCS,), jnp.float32, -0.5, 0.5)
    return (ar_values, ma_values)


def draw_autoreg(key, part):
    ar_values, ma_values = noise_coefficients(key)
    return ar_values.astype(jnp.float32)


def draw_movavg(key, part):
    ar_values, ma_values = noise_coefficients(key)
    return ma_values.astype(jnp.float32)


def shard_levels(stream_key, extent, pieces, low, high):
    gain = 1.0
    for axis_at, parts in pieces:
        draws = jax.random.uniform(jax.random.fold_in(jax.random.fold_in(stream_key, 6), axis_at), (parts,), jnp.float32, low / len(pieces), high / len(pieces))
        gain = gain * jnp.repeat(jnp.exp(draws), extent[axis_at] // parts).reshape((-1,) + (1,) * (len(extent) - 1 - axis_at))
    return gain


def centred(key, extent, width, most, split=(), kind=jnp.bfloat16):
    loudness = shard_levels(key, extent, split, -0.22, 0.18) if split else 1.0
    array = jax.random.normal(key, extent, jnp.float32) * width * loudness
    return jnp.minimum(jnp.maximum(array, -most), most).astype(kind)


def setup_inputs(seed: int = 0) -> dict:
    key_of = jax.random.split(jax.random.key(seed), 7)
    return {
        "design": centred(key_of[0], (ROWS, NC), 1.0, 6.0, ((0, 32), (1, 4))),
        "partials": centred(key_of[1], (ROWS, NA), 0.02, 0.119628906, ((0, 32),)),
        "observed": centred(key_of[2], (ROWS,), 1.0, 6.0, ((0, 32),)),
        "arc_of_row": draw_arc_of_row(jax.random.fold_in(key_of[6], 71), 0),
        "autoreg": draw_autoreg(jax.random.fold_in(key_of[6], 71), 0),
        "movavg": draw_movavg(jax.random.fold_in(key_of[6], 71), 0),
    }


def whiten_matrix(order_row, order_col, usable_row, usable_col, ar_value, ma_value):
    spacing = order_row[:, None] - order_col[None, :]
    lag_steps = jnp.maximum(spacing - 1, 0)
    parity = (lag_steps % 2).astype(jnp.float32)
    flip_sign = 1.0 - 2.0 * parity
    decayed = -(ar_value + ma_value) * flip_sign * jnp.exp(lag_steps.astype(jnp.float32) * jnp.log(ma_value))
    entry = jnp.where(spacing == 0, jnp.float32(1.0), decayed)
    allowed = usable_row[:, None] & usable_col[None, :] & (spacing >= 0)
    return jnp.where(allowed, entry, jnp.float32(0.0)).astype(jnp.bfloat16)

def eliminate(whitener, rows_design, rows_params, rows_obs, scale):
    white_design = jnp.dot(whitener.astype(jnp.float32), rows_design.astype(jnp.float32), preferred_element_type=jnp.float32)
    white_params = jnp.dot(whitener.astype(jnp.float32), rows_params.astype(jnp.float32), preferred_element_type=jnp.float32)
    white_obs = jnp.dot(whitener.astype(jnp.float32), rows_obs.astype(jnp.float32), preferred_element_type=jnp.float32)
    param_count = rows_params.shape[1]
    param_gram = jnp.dot(white_params.T, white_params, precision=lax.Precision.HIGHEST) + jnp.eye(param_count, dtype=jnp.float32)
    factor = jnp.linalg.cholesky(param_gram)
    basis = lax.linalg.triangular_solve(factor, white_params.T, left_side=True, lower=True)
    arc_terms = jnp.dot(basis, white_design, precision=lax.Precision.HIGHEST)
    arc_rhs = jnp.dot(basis, white_obs, precision=lax.Precision.HIGHEST)
    right_part = (jnp.dot(white_design.T, white_obs, precision=lax.Precision.HIGHEST) - jnp.dot(arc_terms.T, arc_rhs, precision=lax.Precision.HIGHEST)) * scale
    return (white_design.astype(jnp.bfloat16), arc_terms.astype(jnp.bfloat16), right_part)

def reference(design, partials, observed, arc_of_row, autoreg, movavg):
    arc_ids = arc_of_row[:, 0]
    pad_design = jnp.concatenate([design, jnp.zeros((1, NC), jnp.bfloat16)], axis=0)
    pad_params = jnp.concatenate([partials, jnp.zeros((1, NA), jnp.bfloat16)], axis=0)
    pad_obs = jnp.concatenate([observed, jnp.zeros((1,), jnp.bfloat16)], axis=0)
    position = jnp.arange(SLOTS, dtype=jnp.int32)
    scale = 1.0 / ROWS

    def one_arc(running, arc_id):
        normal, right_hand = running
        arc_length = jnp.sum((arc_ids == arc_id).astype(jnp.int32))
        arc_start = jnp.sum((arc_ids < arc_id).astype(jnp.int32))
        usable = position < arc_length
        epochs = (arc_start + position).astype(jnp.int32)
        row_index = (epochs % N_TM * ROW_DEV + epochs // N_TM).astype(jnp.int32)
        picked = jnp.where(usable, row_index, jnp.int32(ROWS)).astype(jnp.int32)
        whitener = whiten_matrix(position, position, usable, usable, autoreg[arc_id], movavg[arc_id])
        design_bf, terms_bf, right_part = eliminate(whitener, pad_design[picked], pad_params[picked], pad_obs[picked], scale)
        partial_value = (jnp.dot(design_bf.T.astype(jnp.float32), design_bf.astype(jnp.float32), preferred_element_type=jnp.float32) - jnp.dot(terms_bf.T.astype(jnp.float32), terms_bf.astype(jnp.float32), preferred_element_type=jnp.float32)) * scale
        rounded = lax.optimization_barrier(partial_value.astype(jnp.bfloat16))
        return ((normal + rounded.astype(jnp.float32), right_hand + right_part), None)
    start_state = (jnp.zeros((NC, NC), jnp.float32), jnp.zeros((NC,), jnp.float32))
    (normal, right_hand), _ = lax.scan(one_arc, start_state, jnp.arange(ARCS, dtype=jnp.int32))
    return (normal, right_hand)
```

```python
import jax
import jax.numpy as jnp
from jax import lax
from jax.sharding import Mesh, PartitionSpec as P

TM = ("tmc", "core")


def whiten_matrix(order_row, order_col, usable_row, usable_col, ar_value, ma_value):
    spacing = order_row[:, None] - order_col[None, :]
    lag_steps = jnp.maximum(spacing - 1, 0)
    parity = (lag_steps % 2).astype(jnp.float32)
    flip_sign = 1.0 - 2.0 * parity
    decayed = (
        -(ar_value + ma_value)
        * flip_sign
        * jnp.exp(lag_steps.astype(jnp.float32) * jnp.log(ma_value))
    )
    entry = jnp.where(spacing == 0, jnp.float32(1.0), decayed)
    allowed = usable_row[:, None] & usable_col[None, :] & (spacing >= 0)
    return jnp.where(allowed, entry, jnp.float32(0.0)).astype(jnp.bfloat16)


def eliminate(whitener, rows_design, rows_params, rows_obs, scale):
    white_design = jnp.dot(whitener, rows_design, preferred_element_type=jnp.float32)
    white_params = jnp.dot(whitener, rows_params, preferred_element_type=jnp.float32)
    white_obs = jnp.dot(whitener, rows_obs, preferred_element_type=jnp.float32)
    param_count = rows_params.shape[1]
    param_gram = jnp.dot(white_params.T, white_params, precision=lax.Precision.HIGHEST) + jnp.eye(
        param_count, dtype=jnp.float32
    )
    factor = jnp.linalg.cholesky(param_gram)
    basis = lax.linalg.triangular_solve(factor, white_params.T, left_side=True, lower=True)
    arc_terms = jnp.dot(basis, white_design, precision=lax.Precision.HIGHEST)
    arc_rhs = jnp.dot(basis, white_obs, precision=lax.Precision.HIGHEST)
    right_part = (
        jnp.dot(white_design.T, white_obs, precision=lax.Precision.HIGHEST)
        - jnp.dot(arc_terms.T, arc_rhs, precision=lax.Precision.HIGHEST)
    ) * scale
    return (white_design.astype(jnp.bfloat16), arc_terms.astype(jnp.bfloat16), right_part)


def body(design, partials, observed, arc_of_row, autoreg, movavg):
    chip_count = lax.axis_size("tmc")
    core_count = lax.axis_size("core")
    tile_count = chip_count * core_count
    device_index = lax.axis_index("tmc") * core_count + lax.axis_index("core")
    rows_dev = design.shape[0]
    panel_width = design.shape[1]
    param_count = partials.shape[1]
    capacity = 3 * rows_dev // 2 // tile_count
    slot_count = tile_count * capacity
    scale = 1.0 / (rows_dev * tile_count)
    arc_ids = arc_of_row[:, 0]
    epoch_table = arc_ids.reshape(rows_dev, tile_count)
    local_arcs = lax.dynamic_slice_in_dim(epoch_table, device_index, 1, 1)[:, 0]
    onehot = (local_arcs[:, None] == jnp.arange(tile_count, dtype=jnp.int32)[None, :]).astype(
        jnp.int32
    )
    earlier = jnp.cumsum(onehot, axis=0) - onehot
    within = jnp.sum(earlier * onehot, axis=1)
    target_slot = local_arcs * capacity + within
    source_row = (
        jnp.zeros((slot_count,), jnp.int32)
        .at[target_slot]
        .set(jnp.arange(1, rows_dev + 1, dtype=jnp.int32))
    )

    def pick_rows(values):
        padded = jnp.concatenate([jnp.zeros((1,) + values.shape[1:], values.dtype), values], axis=0)
        return jnp.take(padded, source_row, axis=0)

    send_design = pick_rows(design).reshape(tile_count, capacity, panel_width)
    send_params = pick_rows(partials).reshape(tile_count, capacity, param_count)
    send_obs = pick_rows(observed).reshape(tile_count, capacity)
    got_design, got_params, got_obs = (
        lax.all_to_all(send_design, TM, split_axis=0, concat_axis=0, tiled=True),
        lax.all_to_all(send_params, TM, split_axis=0, concat_axis=0, tiled=True),
        lax.all_to_all(send_obs, TM, split_axis=0, concat_axis=0, tiled=True),
    )
    got_design = got_design.reshape(slot_count, panel_width)
    got_params = got_params.reshape(slot_count, param_count)
    got_obs = got_obs.reshape(slot_count)
    per_source = jnp.sum((epoch_table == device_index).astype(jnp.int32), axis=0)
    arc_start = jnp.sum((arc_ids < device_index).astype(jnp.int32))
    first_pos = jnp.mod(jnp.arange(tile_count, dtype=jnp.int32) - arc_start, tile_count)
    offset_in = jnp.arange(capacity, dtype=jnp.int32)
    order_pos = (first_pos[:, None] + offset_in[None, :] * tile_count).reshape(slot_count)
    usable = (offset_in[None, :] < per_source[:, None]).reshape(slot_count)
    whitener = whiten_matrix(
        order_pos, order_pos, usable, usable, autoreg[device_index], movavg[device_index]
    )
    design_bf, terms_bf, right_part = eliminate(whitener, got_design, got_params, got_obs, scale)
    right_hand = lax.psum(right_part, TM)
    own_rows = jnp.concatenate([design_bf, terms_bf], axis=0)
    signed_rows = jnp.concatenate([design_bf, -terms_bf], axis=0)
    gathered = lax.all_gather(signed_rows, "panel", axis=1, tiled=True)
    coeff_count = gathered.shape[1]
    block_rows = coeff_count // tile_count
    gathered = (
        gathered.reshape(-1, chip_count, core_count, block_rows)
        .transpose(0, 2, 1, 3)
        .reshape(-1, coeff_count)
    )
    product = lax.dot_general(
        gathered, own_rows, (((0,), (0,)), ((), ())), preferred_element_type=jnp.float32
    )
    partial = (product * scale).astype(jnp.bfloat16)
    partial = lax.psum_scatter(partial, "core", scatter_dimension=0, tiled=True)
    normal = lax.psum_scatter(partial, "tmc", scatter_dimension=0, tiled=True).astype(
        jnp.float32
    )
    return (normal, right_hand)


def solution(mesh):
    chips = mesh.devices.shape[0] // 2
    split = Mesh(
        mesh.devices.reshape(chips, 2, mesh.devices.shape[1]), ("tmc", "core", "panel")
    )
    in_specs = (P(TM, "panel"), P(TM, None), P(TM), P(), P(), P())
    out_specs = (P(TM, "panel"), P("panel"))
    return jax.shard_map(body, mesh=split, in_specs=in_specs, out_specs=out_specs, check_vma=False)
```

```python
import jax
import jax.numpy as jnp
from jax import lax
from jax.sharding import PartitionSpec as P


def whiten_matrix(order_row, order_col, usable_row, usable_col, ar_value, ma_value):
    spacing = order_row[:, None] - order_col[None, :]
    lag_steps = jnp.maximum(spacing - 1, 0)
    parity = (lag_steps % 2).astype(jnp.float32)
    flip_sign = 1.0 - 2.0 * parity
    decayed = (
        -(ar_value + ma_value)
        * flip_sign
        * jnp.exp(lag_steps.astype(jnp.float32) * jnp.log(ma_value))
    )
    entry = jnp.where(spacing == 0, jnp.float32(1.0), decayed)
    allowed = usable_row[:, None] & usable_col[None, :] & (spacing >= 0)
    return jnp.where(allowed, entry, jnp.float32(0.0)).astype(jnp.bfloat16)


def eliminate(whitener, rows_design, rows_params, rows_obs, scale):
    white_design = jnp.dot(whitener, rows_design, preferred_element_type=jnp.float32)
    white_params = jnp.dot(whitener, rows_params, preferred_element_type=jnp.float32)
    white_obs = jnp.dot(whitener, rows_obs, preferred_element_type=jnp.float32)
    param_count = rows_params.shape[1]
    param_gram = jnp.dot(white_params.T, white_params, precision=lax.Precision.HIGHEST) + jnp.eye(
        param_count, dtype=jnp.float32
    )
    factor = jnp.linalg.cholesky(param_gram)
    basis = lax.linalg.triangular_solve(factor, white_params.T, left_side=True, lower=True)
    arc_terms = jnp.dot(basis, white_design, precision=lax.Precision.HIGHEST)
    arc_rhs = jnp.dot(basis, white_obs, precision=lax.Precision.HIGHEST)
    right_part = (
        jnp.dot(white_design.T, white_obs, precision=lax.Precision.HIGHEST)
        - jnp.dot(arc_terms.T, arc_rhs, precision=lax.Precision.HIGHEST)
    ) * scale
    return (white_design.astype(jnp.bfloat16), arc_terms.astype(jnp.bfloat16), right_part)


def mirror_pairs(tile_count, panel_count, offset):
    group = tile_count // panel_count
    pairs = []
    for u in range(tile_count):
        for q in range(panel_count):
            target = group * q + (u % group + offset) % group
            pairs.append((u * panel_count + q, target * panel_count + u // group))
    return pairs


def body(design, partials, observed, arc_of_row, autoreg, movavg):
    tile_count = lax.axis_size("tm")
    device_index = lax.axis_index("tm")
    rows_dev = design.shape[0]
    panel_width = design.shape[1]
    param_count = partials.shape[1]
    capacity = 3 * rows_dev // 2 // tile_count
    slot_count = tile_count * capacity
    scale = 1.0 / (rows_dev * tile_count)
    arc_ids = arc_of_row[:, 0]
    epoch_table = arc_ids.reshape(rows_dev, tile_count)
    local_arcs = lax.dynamic_slice_in_dim(epoch_table, device_index, 1, 1)[:, 0]
    onehot = (local_arcs[:, None] == jnp.arange(tile_count, dtype=jnp.int32)[None, :]).astype(
        jnp.int32
    )
    earlier = jnp.cumsum(onehot, axis=0) - onehot
    within = jnp.sum(earlier * onehot, axis=1)
    target_slot = local_arcs * capacity + within
    source_row = (
        jnp.zeros((slot_count,), jnp.int32)
        .at[target_slot]
        .set(jnp.arange(1, rows_dev + 1, dtype=jnp.int32))
    )

    def pick_rows(values):
        padded = jnp.concatenate([jnp.zeros((1,) + values.shape[1:], values.dtype), values], axis=0)
        return jnp.take(padded, source_row, axis=0)

    send_design = pick_rows(design).reshape(tile_count, capacity, panel_width)
    send_params = pick_rows(partials).reshape(tile_count, capacity, param_count)
    send_obs = pick_rows(observed).reshape(tile_count, capacity)
    got_design, got_params, got_obs = (
        lax.all_to_all(send_design, "tm", split_axis=0, concat_axis=0, tiled=True),
        lax.all_to_all(send_params, "tm", split_axis=0, concat_axis=0, tiled=True),
        lax.all_to_all(send_obs, "tm", split_axis=0, concat_axis=0, tiled=True),
    )
    got_design = got_design.reshape(slot_count, panel_width)
    got_params = got_params.reshape(slot_count, param_count)
    got_obs = got_obs.reshape(slot_count)
    per_source = jnp.sum((epoch_table == device_index).astype(jnp.int32), axis=0)
    arc_start = jnp.sum((arc_ids < device_index).astype(jnp.int32))
    first_pos = jnp.mod(jnp.arange(tile_count, dtype=jnp.int32) - arc_start, tile_count)
    offset_in = jnp.arange(capacity, dtype=jnp.int32)
    order_pos = (first_pos[:, None] + offset_in[None, :] * tile_count).reshape(slot_count)
    usable = (offset_in[None, :] < per_source[:, None]).reshape(slot_count)
    whitener = whiten_matrix(
        order_pos, order_pos, usable, usable, autoreg[device_index], movavg[device_index]
    )
    design_bf, terms_bf, right_part = eliminate(whitener, got_design, got_params, got_obs, scale)
    right_hand = lax.psum(right_part, "tm")
    own_rows = jnp.concatenate([design_bf, terms_bf], axis=0)
    signed_rows = jnp.concatenate([design_bf, -terms_bf], axis=0)
    gathered = lax.all_gather(signed_rows, "panel", axis=1, tiled=True)
    panel_count = lax.axis_size("panel")
    panel_index = lax.axis_index("panel")
    group = tile_count // panel_count
    width = panel_width // group
    kept = group // 2 + 1
    row_count = gathered.shape[0]
    doubled = jnp.concatenate([own_rows, own_rows[:, : (kept - 1) * width]], axis=1)
    windows = jnp.stack(
        [doubled[:, k * width : (k + kept) * width] for k in range(group)]
    )
    row_tiles = gathered.reshape(row_count, panel_count, group, width)
    pieces = []
    for r in range(panel_count):
        block = lax.dot_general(
            row_tiles[:, r], windows, (((0,), (1,)), ((1,), (0,))),
            preferred_element_type=jnp.float32,
        )
        pieces.append((block * scale).astype(jnp.bfloat16))
    stacked = jnp.concatenate(pieces, axis=0).reshape(tile_count * width, kept * width)
    reduced = lax.psum_scatter(stacked, "tm", scatter_dimension=0, tiled=True).astype(
        jnp.float32
    )
    tiles = [reduced[:, s * width : (s + 1) * width] for s in range(kept)]
    for s in range(kept, group):
        mirror = group - s
        sent = reduced[:, mirror * width : (mirror + 1) * width].T
        tiles.append(lax.ppermute(sent, ("tm", "panel"), mirror_pairs(tile_count, panel_count, group - s)))
    by_offset = jnp.stack(tiles, axis=0)
    by_offset = jnp.concatenate([by_offset, by_offset], axis=0)
    start = (group - device_index % group) % group
    ordered = lax.dynamic_slice_in_dim(by_offset, start, group, 0)
    normal = ordered.transpose(1, 0, 2).reshape(width, group * width)
    return (normal, right_hand)


def solution(mesh):
    in_specs = (P("tm", "panel"), P("tm", None), P("tm"), P(), P(), P())
    out_specs = (P("tm", "panel"), P("panel"))
    return jax.shard_map(body, mesh=mesh, in_specs=in_specs, out_specs=out_specs, check_vma=False)
```

```python
import functools

import jax
import jax.numpy as jnp
from jax import lax
from jax.experimental import pallas as pl
from jax.sharding import PartitionSpec as P


def whiten_matrix(order_row, order_col, usable_row, usable_col, ar_value, ma_value):
    spacing = order_row[:, None] - order_col[None, :]
    lag_steps = jnp.maximum(spacing - 1, 0)
    parity = (lag_steps % 2).astype(jnp.float32)
    flip_sign = 1.0 - 2.0 * parity
    decayed = (
        -(ar_value + ma_value)
        * flip_sign
        * jnp.exp(lag_steps.astype(jnp.float32) * jnp.log(ma_value))
    )
    entry = jnp.where(spacing == 0, jnp.float32(1.0), decayed)
    allowed = usable_row[:, None] & usable_col[None, :] & (spacing >= 0)
    return jnp.where(allowed, entry, jnp.float32(0.0)).astype(jnp.bfloat16)


def eliminate(whitener, rows_design, rows_params, rows_obs, scale):
    white_design = jnp.dot(whitener, rows_design, preferred_element_type=jnp.float32)
    white_params = jnp.dot(whitener, rows_params, preferred_element_type=jnp.float32)
    white_obs = jnp.dot(whitener, rows_obs, preferred_element_type=jnp.float32)
    param_count = rows_params.shape[1]
    param_gram = jnp.dot(white_params.T, white_params, precision=lax.Precision.HIGHEST) + jnp.eye(
        param_count, dtype=jnp.float32
    )
    factor = jnp.linalg.cholesky(param_gram)
    basis = lax.linalg.triangular_solve(factor, white_params.T, left_side=True, lower=True)
    arc_terms = jnp.dot(basis, white_design, precision=lax.Precision.HIGHEST)
    arc_rhs = jnp.dot(basis, white_obs, precision=lax.Precision.HIGHEST)
    right_part = (
        jnp.dot(white_design.T, white_obs, precision=lax.Precision.HIGHEST)
        - jnp.dot(arc_terms.T, arc_rhs, precision=lax.Precision.HIGHEST)
    ) * scale
    return (white_design.astype(jnp.bfloat16), arc_terms.astype(jnp.bfloat16), right_part)


def window_kernel(group, width, kept, scale, rows_ref, cols_ref, rider_ref, out_ref):
    tile = pl.program_id(0)
    start = pl.multiple_of((tile % group) * width, 16)
    window = cols_ref[pl.ds(start, kept * width), :]
    product = lax.dot_general(
        rows_ref[...], window, (((1,), (1,)), ((), ())), preferred_element_type=jnp.float32
    )
    out_ref[:width, :] = (product * scale).astype(out_ref.dtype)
    out_ref[width:, :] = rider_ref[...]


def window_products(rows, cols, riders, group, width, kept, scale):
    tile_count = rows.shape[0] // width
    depth = rows.shape[1]
    chunk = width + riders.shape[0]
    return pl.pallas_call(
        functools.partial(window_kernel, group, width, kept, scale),
        out_shape=jax.ShapeDtypeStruct((tile_count * chunk, kept * width), jnp.bfloat16),
        grid=(tile_count,),
        in_specs=[
            pl.BlockSpec((width, depth), lambda t: (t, 0)),
            pl.BlockSpec(cols.shape, lambda t: (0, 0)),
            pl.BlockSpec(riders.shape, lambda t: (0, 0)),
        ],
        out_specs=pl.BlockSpec((chunk, kept * width), lambda t: (t, 0)),
        cost_estimate=pl.CostEstimate(
            flops=2 * tile_count * width * kept * width * depth,
            bytes_accessed=2 * (rows.size + cols.size + tile_count * chunk * kept * width),
            transcendentals=0,
        ),
    )(rows, cols, riders)


def mirror_pairs(tile_count, panel_count, offset):
    group = tile_count // panel_count
    pairs = []
    for u in range(tile_count):
        for q in range(panel_count):
            target = group * q + (u % group + offset) % group
            pairs.append((u * panel_count + q, target * panel_count + u // group))
    return pairs


def body(design, partials, observed, arc_of_row, autoreg, movavg):
    tile_count = lax.axis_size("tm")
    device_index = lax.axis_index("tm")
    rows_dev = design.shape[0]
    panel_width = design.shape[1]
    param_count = partials.shape[1]
    capacity = 3 * rows_dev // 2 // tile_count
    slot_count = tile_count * capacity
    scale = 1.0 / (rows_dev * tile_count)
    arc_ids = arc_of_row[:, 0]
    epoch_table = arc_ids.reshape(rows_dev, tile_count)
    local_arcs = lax.dynamic_slice_in_dim(epoch_table, device_index, 1, 1)[:, 0]
    onehot = (local_arcs[:, None] == jnp.arange(tile_count, dtype=jnp.int32)[None, :]).astype(
        jnp.int32
    )
    earlier = jnp.cumsum(onehot, axis=0) - onehot
    within = jnp.sum(earlier * onehot, axis=1)
    target_slot = local_arcs * capacity + within
    source_row = (
        jnp.zeros((slot_count,), jnp.int32)
        .at[target_slot]
        .set(jnp.arange(1, rows_dev + 1, dtype=jnp.int32))
    )

    def pick_rows(values):
        padded = jnp.concatenate([jnp.zeros((1,) + values.shape[1:], values.dtype), values], axis=0)
        return jnp.take(padded, source_row, axis=0)

    send_design = pick_rows(design).reshape(tile_count, capacity, panel_width)
    send_params = pick_rows(partials).reshape(tile_count, capacity, param_count)
    send_obs = pick_rows(observed).reshape(tile_count, capacity)
    got_design, got_params, got_obs = (
        lax.all_to_all(send_design, "tm", split_axis=0, concat_axis=0, tiled=True),
        lax.all_to_all(send_params, "tm", split_axis=0, concat_axis=0, tiled=True),
        lax.all_to_all(send_obs, "tm", split_axis=0, concat_axis=0, tiled=True),
    )
    got_design = got_design.reshape(slot_count, panel_width)
    got_params = got_params.reshape(slot_count, param_count)
    got_obs = got_obs.reshape(slot_count)
    per_source = jnp.sum((epoch_table == device_index).astype(jnp.int32), axis=0)
    arc_start = jnp.sum((arc_ids < device_index).astype(jnp.int32))
    first_pos = jnp.mod(jnp.arange(tile_count, dtype=jnp.int32) - arc_start, tile_count)
    offset_in = jnp.arange(capacity, dtype=jnp.int32)
    order_pos = (first_pos[:, None] + offset_in[None, :] * tile_count).reshape(slot_count)
    usable = (offset_in[None, :] < per_source[:, None]).reshape(slot_count)
    whitener = whiten_matrix(
        order_pos, order_pos, usable, usable, autoreg[device_index], movavg[device_index]
    )
    design_bf, terms_bf, right_part = eliminate(whitener, got_design, got_params, got_obs, scale)
    own_rows = jnp.concatenate([design_bf, terms_bf], axis=0).T
    signed_rows = jnp.concatenate([design_bf, -terms_bf], axis=0).T
    gathered = lax.all_gather(signed_rows, "panel", axis=0, tiled=True)
    panel_count = lax.axis_size("panel")
    group = tile_count // panel_count
    width = panel_width // group
    kept = group // 2 + 1
    doubled = jnp.concatenate([own_rows, own_rows[: (kept - 1) * width]], axis=0)
    spare = 8
    riders = jnp.zeros((spare * kept * width,), jnp.float32).at[: right_part.shape[0]].set(right_part)
    riders = riders.reshape(spare, kept * width).astype(jnp.bfloat16)
    stacked = window_products(gathered, doubled, riders, group, width, kept, scale)
    summed = lax.psum_scatter(stacked, "tm", scatter_dimension=0, tiled=True).astype(
        jnp.float32
    )
    reduced = summed[:width]
    right_hand = summed[width:].reshape(-1)[: right_part.shape[0]]
    tiles = [reduced[:, s * width : (s + 1) * width] for s in range(kept)]
    for s in range(kept, group):
        mirror = group - s
        sent = reduced[:, mirror * width : (mirror + 1) * width].T
        tiles.append(lax.ppermute(sent, ("tm", "panel"), mirror_pairs(tile_count, panel_count, group - s)))
    by_offset = jnp.stack(tiles, axis=0)
    by_offset = jnp.concatenate([by_offset, by_offset], axis=0)
    start = (group - device_index % group) % group
    ordered = lax.dynamic_slice_in_dim(by_offset, start, group, 0)
    normal = ordered.transpose(1, 0, 2).reshape(width, group * width)
    return (normal, right_hand)


def solution(mesh):
    in_specs = (P("tm", "panel"), P("tm", None), P("tm"), P(), P(), P())
    out_specs = (P("tm", "panel"), P("panel"))
    return jax.shard_map(body, mesh=mesh, in_specs=in_specs, out_specs=out_specs, check_vma=False)
```

```python
import jax
import jax.numpy as jnp
from jax import lax
from jax.sharding import Mesh, PartitionSpec as P

TM = ("tmc", "core")


def whiten_matrix(order_row, order_col, usable_row, usable_col, ar_value, ma_value):
    spacing = order_row[:, None] - order_col[None, :]
    lag_steps = jnp.maximum(spacing - 1, 0)
    parity = (lag_steps % 2).astype(jnp.float32)
    flip_sign = 1.0 - 2.0 * parity
    decayed = (
        -(ar_value + ma_value)
        * flip_sign
        * jnp.exp(lag_steps.astype(jnp.float32) * jnp.log(ma_value))
    )
    entry = jnp.where(spacing == 0, jnp.float32(1.0), decayed)
    allowed = usable_row[:, None] & usable_col[None, :] & (spacing >= 0)
    return jnp.where(allowed, entry, jnp.float32(0.0)).astype(jnp.bfloat16)


def eliminate(whitener, rows_design, rows_params, rows_obs, scale):
    white_design = jnp.dot(whitener, rows_design, preferred_element_type=jnp.float32)
    white_params = jnp.dot(whitener, rows_params, preferred_element_type=jnp.float32)
    white_obs = jnp.dot(whitener, rows_obs, preferred_element_type=jnp.float32)
    param_count = rows_params.shape[1]
    param_gram = jnp.dot(white_params.T, white_params, precision=lax.Precision.HIGHEST) + jnp.eye(
        param_count, dtype=jnp.float32
    )
    factor = jnp.linalg.cholesky(param_gram)
    basis = lax.linalg.triangular_solve(factor, white_params.T, left_side=True, lower=True)
    arc_terms = jnp.dot(basis, white_design, precision=lax.Precision.HIGHEST)
    arc_rhs = jnp.dot(basis, white_obs, precision=lax.Precision.HIGHEST)
    right_part = (
        jnp.dot(white_design.T, white_obs, precision=lax.Precision.HIGHEST)
        - jnp.dot(arc_terms.T, arc_rhs, precision=lax.Precision.HIGHEST)
    ) * scale
    return (white_design.astype(jnp.bfloat16), arc_terms.astype(jnp.bfloat16), right_part)


def body(design, partials, observed, arc_of_row, autoreg, movavg):
    chip_count = lax.axis_size("tmc")
    core_count = lax.axis_size("core")
    core_index = lax.axis_index("core")
    tile_count = chip_count * core_count
    device_index = lax.axis_index("tmc") * core_count + core_index
    rows_dev = design.shape[0]
    panel_width = design.shape[1]
    param_count = partials.shape[1]
    capacity = 3 * rows_dev // 2 // tile_count
    slot_count = tile_count * capacity
    scale = 1.0 / (rows_dev * tile_count)
    arc_ids = arc_of_row[:, 0]
    epoch_table = arc_ids.reshape(rows_dev, tile_count)
    local_arcs = lax.dynamic_slice_in_dim(epoch_table, device_index, 1, 1)[:, 0]
    onehot = (local_arcs[:, None] == jnp.arange(tile_count, dtype=jnp.int32)[None, :]).astype(
        jnp.int32
    )
    earlier = jnp.cumsum(onehot, axis=0) - onehot
    within = jnp.sum(earlier * onehot, axis=1)
    target_slot = local_arcs * capacity + within
    source_row = (
        jnp.zeros((slot_count,), jnp.int32)
        .at[target_slot]
        .set(jnp.arange(1, rows_dev + 1, dtype=jnp.int32))
    )

    def pick_rows(values):
        padded = jnp.concatenate([jnp.zeros((1,) + values.shape[1:], values.dtype), values], axis=0)
        return jnp.take(padded, source_row, axis=0)

    send_design = pick_rows(design).reshape(tile_count, capacity, panel_width)
    send_params = pick_rows(partials).reshape(tile_count, capacity, param_count)
    send_obs = pick_rows(observed).reshape(tile_count, capacity)
    got_design, got_params, got_obs = (
        lax.all_to_all(send_design, TM, split_axis=0, concat_axis=0, tiled=True),
        lax.all_to_all(send_params, TM, split_axis=0, concat_axis=0, tiled=True),
        lax.all_to_all(send_obs, TM, split_axis=0, concat_axis=0, tiled=True),
    )
    got_design = got_design.reshape(slot_count, panel_width)
    got_params = got_params.reshape(slot_count, param_count)
    got_obs = got_obs.reshape(slot_count)
    per_source = jnp.sum((epoch_table == device_index).astype(jnp.int32), axis=0)
    arc_start = jnp.sum((arc_ids < device_index).astype(jnp.int32))
    first_pos = jnp.mod(jnp.arange(tile_count, dtype=jnp.int32) - arc_start, tile_count)
    offset_in = jnp.arange(capacity, dtype=jnp.int32)
    order_pos = (first_pos[:, None] + offset_in[None, :] * tile_count).reshape(slot_count)
    usable = (offset_in[None, :] < per_source[:, None]).reshape(slot_count)
    whitener = whiten_matrix(
        order_pos, order_pos, usable, usable, autoreg[device_index], movavg[device_index]
    )
    design_bf, terms_bf, right_part = eliminate(whitener, got_design, got_params, got_obs, scale)
    right_hand = lax.psum(right_part, TM)
    own_rows = jnp.concatenate([design_bf, terms_bf], axis=0)
    signed_rows = jnp.concatenate([design_bf, -terms_bf], axis=0).T
    gathered = lax.all_gather(signed_rows, "panel", axis=0, tiled=True)
    block_rows = gathered.shape[0] // tile_count
    by_core = gathered.reshape(chip_count, core_count, block_rows, gathered.shape[1])
    swap = [(0, 1), (1, 0)]
    kept_rows = lax.dynamic_index_in_dim(by_core, core_index, 1, keepdims=False)
    given_rows = lax.dynamic_index_in_dim(by_core, 1 - core_index, 1, keepdims=False)
    got_rows = lax.ppermute(given_rows, "core", swap)
    got_cols = lax.ppermute(own_rows, "core", swap)
    row_side = jnp.concatenate([kept_rows, got_rows], axis=2).reshape(
        chip_count * block_rows, -1
    )
    col_side = jnp.concatenate([own_rows, got_cols], axis=0)
    product = jnp.dot(row_side, col_side, preferred_element_type=jnp.float32)
    normal = lax.psum_scatter(
        (product * scale).astype(jnp.bfloat16), "tmc", scatter_dimension=0, tiled=True
    ).astype(jnp.float32)
    return (normal, right_hand)


def solution(mesh):
    chips = mesh.devices.shape[0] // 2
    split = Mesh(
        mesh.devices.reshape(chips, 2, mesh.devices.shape[1]), ("tmc", "core", "panel")
    )
    in_specs = (P(TM, "panel"), P(TM, None), P(TM), P(), P(), P())
    out_specs = (P(TM, "panel"), P("panel"))
    return jax.shard_map(body, mesh=split, in_specs=in_specs, out_specs=out_specs, check_vma=False)
```

```python
import jax
import jax.numpy as jnp
from jax import lax
from jax.sharding import Mesh, PartitionSpec as P

TM = ("tmc", "core")


def whiten_matrix(order_row, order_col, usable_row, usable_col, ar_value, ma_value):
    spacing = order_row[:, None] - order_col[None, :]
    lag_steps = jnp.maximum(spacing - 1, 0)
    parity = (lag_steps % 2).astype(jnp.float32)
    flip_sign = 1.0 - 2.0 * parity
    decayed = (
        -(ar_value + ma_value)
        * flip_sign
        * jnp.exp(lag_steps.astype(jnp.float32) * jnp.log(ma_value))
    )
    entry = jnp.where(spacing == 0, jnp.float32(1.0), decayed)
    allowed = usable_row[:, None] & usable_col[None, :] & (spacing >= 0)
    return jnp.where(allowed, entry, jnp.float32(0.0)).astype(jnp.bfloat16)


def eliminate(whitener, rows_design, rows_params, rows_obs, scale):
    white_design = jnp.dot(whitener, rows_design, preferred_element_type=jnp.float32)
    white_params = jnp.dot(whitener, rows_params, preferred_element_type=jnp.float32)
    white_obs = jnp.dot(whitener, rows_obs, preferred_element_type=jnp.float32)
    param_count = rows_params.shape[1]
    param_gram = jnp.dot(white_params.T, white_params, precision=lax.Precision.HIGHEST) + jnp.eye(
        param_count, dtype=jnp.float32
    )
    factor = jnp.linalg.cholesky(param_gram)
    basis = lax.linalg.triangular_solve(factor, white_params.T, left_side=True, lower=True)
    arc_terms = jnp.dot(basis, white_design, precision=lax.Precision.HIGHEST)
    arc_rhs = jnp.dot(basis, white_obs, precision=lax.Precision.HIGHEST)
    right_part = (
        jnp.dot(white_design.T, white_obs, precision=lax.Precision.HIGHEST)
        - jnp.dot(arc_terms.T, arc_rhs, precision=lax.Precision.HIGHEST)
    ) * scale
    return (white_design.astype(jnp.bfloat16), arc_terms.astype(jnp.bfloat16), right_part)


def body(design, partials, observed, arc_of_row, autoreg, movavg):
    chip_count = lax.axis_size("tmc")
    core_count = lax.axis_size("core")
    core_index = lax.axis_index("core")
    tile_count = chip_count * core_count
    device_index = lax.axis_index("tmc") * core_count + core_index
    rows_dev = design.shape[0]
    panel_width = design.shape[1]
    param_count = partials.shape[1]
    capacity = 3 * rows_dev // 2 // tile_count
    slot_count = tile_count * capacity
    scale = 1.0 / (rows_dev * tile_count)
    arc_ids = arc_of_row[:, 0]
    epoch_table = arc_ids.reshape(rows_dev, tile_count)
    local_arcs = lax.dynamic_slice_in_dim(epoch_table, device_index, 1, 1)[:, 0]
    onehot = (local_arcs[:, None] == jnp.arange(tile_count, dtype=jnp.int32)[None, :]).astype(
        jnp.int32
    )
    earlier = jnp.cumsum(onehot, axis=0) - onehot
    within = jnp.sum(earlier * onehot, axis=1)
    target_slot = local_arcs * capacity + within
    source_row = (
        jnp.zeros((slot_count,), jnp.int32)
        .at[target_slot]
        .set(jnp.arange(1, rows_dev + 1, dtype=jnp.int32))
    )

    def pick_rows(values):
        padded = jnp.concatenate([jnp.zeros((1,) + values.shape[1:], values.dtype), values], axis=0)
        return jnp.take(padded, source_row, axis=0)

    send_design = pick_rows(design).reshape(tile_count, capacity, panel_width)
    send_params = pick_rows(partials).reshape(tile_count, capacity, param_count)
    send_obs = pick_rows(observed).reshape(tile_count, capacity)
    got_design, got_params, got_obs = (
        lax.all_to_all(send_design, TM, split_axis=0, concat_axis=0, tiled=True),
        lax.all_to_all(send_params, TM, split_axis=0, concat_axis=0, tiled=True),
        lax.all_to_all(send_obs, TM, split_axis=0, concat_axis=0, tiled=True),
    )
    got_design = got_design.reshape(slot_count, panel_width)
    got_params = got_params.reshape(slot_count, param_count)
    got_obs = got_obs.reshape(slot_count)
    per_source = jnp.sum((epoch_table == device_index).astype(jnp.int32), axis=0)
    arc_start = jnp.sum((arc_ids < device_index).astype(jnp.int32))
    first_pos = jnp.mod(jnp.arange(tile_count, dtype=jnp.int32) - arc_start, tile_count)
    offset_in = jnp.arange(capacity, dtype=jnp.int32)
    order_pos = (first_pos[:, None] + offset_in[None, :] * tile_count).reshape(slot_count)
    usable = (offset_in[None, :] < per_source[:, None]).reshape(slot_count)
    whitener = whiten_matrix(
        order_pos, order_pos, usable, usable, autoreg[device_index], movavg[device_index]
    )
    design_bf, terms_bf, right_part = eliminate(whitener, got_design, got_params, got_obs, scale)
    right_hand = lax.psum(right_part, TM)
    own_rows = jnp.concatenate([design_bf, terms_bf], axis=0)
    signed_rows = jnp.concatenate([design_bf, -terms_bf], axis=0)
    gathered = lax.all_gather(signed_rows, "panel", axis=1, tiled=True)
    gathered, right_hand = lax.optimization_barrier((gathered, right_hand))
    swap = [(0, 1), (1, 0)]
    half = panel_width // core_count
    got_rows = lax.ppermute(gathered, "core", swap)
    got_cols = lax.ppermute(own_rows, "core", swap)
    row_side = jnp.concatenate([gathered, got_rows], axis=0)
    col_side = lax.dynamic_slice_in_dim(
        jnp.concatenate([own_rows, got_cols], axis=0), core_index * half, half, 1
    )
    product = lax.dot_general(
        row_side, col_side, (((0,), (0,)), ((), ())), preferred_element_type=jnp.float32
    )
    pair = lax.psum_scatter(
        (product * scale).astype(jnp.bfloat16), "tmc", scatter_dimension=0, tiled=True
    ).astype(jnp.float32)
    block_rows = pair.shape[0] // core_count
    by_core = pair.reshape(core_count, block_rows, half)
    mine = lax.dynamic_index_in_dim(by_core, core_index, 0, keepdims=False)
    given = lax.dynamic_index_in_dim(by_core, 1 - core_index, 0, keepdims=False)
    got = lax.ppermute(given, "core", swap)
    normal = jnp.where(
        core_index == 0,
        jnp.concatenate([mine, got], axis=1),
        jnp.concatenate([got, mine], axis=1),
    )
    return (normal, right_hand)


def solution(mesh):
    chips = mesh.devices.shape[0] // 2
    split = Mesh(
        mesh.devices.reshape(chips, 2, mesh.devices.shape[1]), ("tmc", "core", "panel")
    )
    in_specs = (P(TM, "panel"), P(TM, None), P(TM), P(), P(), P())
    out_specs = (P(TM, "panel"), P("panel"))
    return jax.shard_map(body, mesh=split, in_specs=in_specs, out_specs=out_specs, check_vma=False)
```

```python
import jax
import jax.numpy as jnp
from jax import lax
from jax.sharding import Mesh, PartitionSpec as P

TM = ("tmc", "core")


def whiten_matrix(order_row, order_col, usable_row, usable_col, ar_value, ma_value):
    spacing = order_row[:, None] - order_col[None, :]
    lag_steps = jnp.maximum(spacing - 1, 0)
    parity = (lag_steps % 2).astype(jnp.float32)
    flip_sign = 1.0 - 2.0 * parity
    decayed = (
        -(ar_value + ma_value)
        * flip_sign
        * jnp.exp(lag_steps.astype(jnp.float32) * jnp.log(ma_value))
    )
    entry = jnp.where(spacing == 0, jnp.float32(1.0), decayed)
    allowed = usable_row[:, None] & usable_col[None, :] & (spacing >= 0)
    return jnp.where(allowed, entry, jnp.float32(0.0)).astype(jnp.bfloat16)


def eliminate(whitener, rows_design, rows_params, rows_obs, scale):
    white_design = jnp.dot(whitener, rows_design, preferred_element_type=jnp.float32)
    white_params = jnp.dot(whitener, rows_params, preferred_element_type=jnp.float32)
    white_obs = jnp.dot(whitener, rows_obs, preferred_element_type=jnp.float32)
    param_count = rows_params.shape[1]
    param_gram = jnp.dot(white_params.T, white_params, precision=lax.Precision.HIGHEST) + jnp.eye(
        param_count, dtype=jnp.float32
    )
    factor = jnp.linalg.cholesky(param_gram)
    basis = lax.linalg.triangular_solve(factor, white_params.T, left_side=True, lower=True)
    arc_terms = jnp.dot(basis, white_design, precision=lax.Precision.HIGHEST)
    arc_rhs = jnp.dot(basis, white_obs, precision=lax.Precision.HIGHEST)
    right_part = (
        jnp.dot(white_design.T, white_obs, precision=lax.Precision.HIGHEST)
        - jnp.dot(arc_terms.T, arc_rhs, precision=lax.Precision.HIGHEST)
    ) * scale
    return (white_design.astype(jnp.bfloat16), arc_terms.astype(jnp.bfloat16), right_part)


def body(design, partials, observed, arc_of_row, autoreg, movavg):
    chip_count = lax.axis_size("tmc")
    core_count = lax.axis_size("core")
    core_index = lax.axis_index("core")
    tile_count = chip_count * core_count
    device_index = lax.axis_index("tmc") * core_count + core_index
    rows_dev = design.shape[0]
    panel_width = design.shape[1]
    param_count = partials.shape[1]
    capacity = 3 * rows_dev // 2 // tile_count
    slot_count = tile_count * capacity
    scale = 1.0 / (rows_dev * tile_count)
    arc_ids = arc_of_row[:, 0]
    epoch_table = arc_ids.reshape(rows_dev, tile_count)
    local_arcs = lax.dynamic_slice_in_dim(epoch_table, device_index, 1, 1)[:, 0]
    onehot = (local_arcs[:, None] == jnp.arange(tile_count, dtype=jnp.int32)[None, :]).astype(
        jnp.int32
    )
    earlier = jnp.cumsum(onehot, axis=0) - onehot
    within = jnp.sum(earlier * onehot, axis=1)
    target_slot = local_arcs * capacity + within
    source_row = (
        jnp.zeros((slot_count,), jnp.int32)
        .at[target_slot]
        .set(jnp.arange(1, rows_dev + 1, dtype=jnp.int32))
    )

    def pick_rows(values):
        padded = jnp.concatenate([jnp.zeros((1,) + values.shape[1:], values.dtype), values], axis=0)
        return jnp.take(padded, source_row, axis=0)

    send_design = pick_rows(design).reshape(tile_count, capacity, panel_width)
    with_obs = jnp.concatenate([partials, observed[:, None]], axis=1)
    send_params = pick_rows(with_obs).reshape(tile_count, capacity, param_count + 1)
    got_design, got_params = (
        lax.all_to_all(send_design, TM, split_axis=0, concat_axis=0, tiled=True),
        lax.all_to_all(send_params, TM, split_axis=0, concat_axis=0, tiled=True),
    )
    got_design = got_design.reshape(slot_count, panel_width)
    got_params = got_params.reshape(slot_count, param_count + 1)
    got_obs = got_params[:, param_count]
    got_params = got_params[:, :param_count]
    per_source = jnp.sum((epoch_table == device_index).astype(jnp.int32), axis=0)
    arc_start = jnp.sum((arc_ids < device_index).astype(jnp.int32))
    first_pos = jnp.mod(jnp.arange(tile_count, dtype=jnp.int32) - arc_start, tile_count)
    offset_in = jnp.arange(capacity, dtype=jnp.int32)
    order_pos = (first_pos[:, None] + offset_in[None, :] * tile_count).reshape(slot_count)
    usable = (offset_in[None, :] < per_source[:, None]).reshape(slot_count)
    whitener = whiten_matrix(
        order_pos, order_pos, usable, usable, autoreg[device_index], movavg[device_index]
    )
    design_bf, terms_bf, right_part = eliminate(whitener, got_design, got_params, got_obs, scale)
    swap = [(0, 1), (1, 0)]
    right_hand = lax.psum(right_part + lax.ppermute(right_part, "core", swap), "tmc")
    own_rows = jnp.concatenate([design_bf, terms_bf], axis=0)
    signed_rows = jnp.concatenate([design_bf, -terms_bf], axis=0)
    gathered = lax.all_gather(signed_rows, "panel", axis=1, tiled=True)
    gathered, right_hand = lax.optimization_barrier((gathered, right_hand))
    half = panel_width // core_count
    got_rows = lax.ppermute(gathered, "core", swap)
    got_cols = lax.ppermute(own_rows, "core", swap)
    row_side = jnp.concatenate([gathered, got_rows], axis=0)
    col_side = lax.dynamic_slice_in_dim(
        jnp.concatenate([own_rows, got_cols], axis=0), core_index * half, half, 1
    )
    product = lax.dot_general(
        row_side, col_side, (((0,), (0,)), ((), ())), preferred_element_type=jnp.float32
    )
    pair = lax.psum_scatter(
        (product * scale).astype(jnp.bfloat16), "tmc", scatter_dimension=0, tiled=True
    ).astype(jnp.float32)
    block_rows = pair.shape[0] // core_count
    by_core = pair.reshape(core_count, block_rows, half)
    mine = lax.dynamic_index_in_dim(by_core, core_index, 0, keepdims=False)
    given = lax.dynamic_index_in_dim(by_core, 1 - core_index, 0, keepdims=False)
    got = lax.ppermute(given, "core", swap)
    normal = jnp.where(
        core_index == 0,
        jnp.concatenate([mine, got], axis=1),
        jnp.concatenate([got, mine], axis=1),
    )
    return (normal, right_hand)


def solution(mesh):
    chips = mesh.devices.shape[0] // 2
    split = Mesh(
        mesh.devices.reshape(chips, 2, mesh.devices.shape[1]), ("tmc", "core", "panel")
    )
    in_specs = (P(TM, "panel"), P(TM, None), P(TM), P(), P(), P())
    out_specs = (P(TM, "panel"), P("panel"))
    return jax.shard_map(body, mesh=split, in_specs=in_specs, out_specs=out_specs, check_vma=False)
```

```python
import jax
import jax.numpy as jnp
from jax import lax
from jax.sharding import Mesh, PartitionSpec as P

TM = ("tmc", "core")


def whiten_matrix(order_row, order_col, usable_row, usable_col, ar_value, ma_value):
    spacing = order_row[:, None] - order_col[None, :]
    lag_steps = jnp.maximum(spacing - 1, 0)
    parity = (lag_steps % 2).astype(jnp.float32)
    flip_sign = 1.0 - 2.0 * parity
    decayed = (
        -(ar_value + ma_value)
        * flip_sign
        * jnp.exp(lag_steps.astype(jnp.float32) * jnp.log(ma_value))
    )
    entry = jnp.where(spacing == 0, jnp.float32(1.0), decayed)
    allowed = usable_row[:, None] & usable_col[None, :] & (spacing >= 0)
    return jnp.where(allowed, entry, jnp.float32(0.0)).astype(jnp.bfloat16)


def eliminate(whitener, rows_design, rows_params, rows_obs, scale):
    white_design = jnp.dot(whitener, rows_design, preferred_element_type=jnp.float32)
    white_params = jnp.dot(whitener, rows_params, preferred_element_type=jnp.float32)
    white_obs = jnp.dot(whitener, rows_obs, preferred_element_type=jnp.float32)
    param_count = rows_params.shape[1]
    param_gram = jnp.dot(white_params.T, white_params, precision=lax.Precision.HIGHEST) + jnp.eye(
        param_count, dtype=jnp.float32
    )
    factor = jnp.linalg.cholesky(param_gram)
    basis = lax.linalg.triangular_solve(factor, white_params.T, left_side=True, lower=True)
    arc_terms = jnp.dot(basis, white_design, precision=lax.Precision.HIGHEST)
    arc_rhs = jnp.dot(basis, white_obs, precision=lax.Precision.HIGHEST)
    right_part = (
        jnp.dot(white_design.T, white_obs, precision=lax.Precision.HIGHEST)
        - jnp.dot(arc_terms.T, arc_rhs, precision=lax.Precision.HIGHEST)
    ) * scale
    return (white_design.astype(jnp.bfloat16), arc_terms.astype(jnp.bfloat16), right_part)


def body(design, partials, observed, arc_of_row, autoreg, movavg):
    chip_count = lax.axis_size("tmc")
    core_count = lax.axis_size("core")
    core_index = lax.axis_index("core")
    tile_count = chip_count * core_count
    device_index = lax.axis_index("tmc") * core_count + core_index
    rows_dev = design.shape[0]
    panel_width = design.shape[1]
    param_count = partials.shape[1]
    capacity = 3 * rows_dev // 2 // tile_count
    slot_count = tile_count * capacity
    scale = 1.0 / (rows_dev * tile_count)
    arc_ids = arc_of_row[:, 0]
    epoch_table = arc_ids.reshape(rows_dev, tile_count)
    local_arcs = lax.dynamic_slice_in_dim(epoch_table, device_index, 1, 1)[:, 0]
    onehot = (local_arcs[:, None] == jnp.arange(tile_count, dtype=jnp.int32)[None, :]).astype(
        jnp.int32
    )
    earlier = jnp.cumsum(onehot, axis=0) - onehot
    within = jnp.sum(earlier * onehot, axis=1)
    target_slot = local_arcs * capacity + within
    source_row = (
        jnp.zeros((slot_count,), jnp.int32)
        .at[target_slot]
        .set(jnp.arange(1, rows_dev + 1, dtype=jnp.int32))
    )

    def pick_rows(values):
        padded = jnp.concatenate([jnp.zeros((1,) + values.shape[1:], values.dtype), values], axis=0)
        return jnp.take(padded, source_row, axis=0)

    send_design = pick_rows(design).reshape(tile_count, capacity, panel_width)
    with_obs = jnp.concatenate([partials, observed[:, None]], axis=1)
    send_params = pick_rows(with_obs).reshape(tile_count, capacity, param_count + 1)
    got_design, got_params = (
        lax.all_to_all(send_design, TM, split_axis=0, concat_axis=0, tiled=True),
        lax.all_to_all(send_params, TM, split_axis=0, concat_axis=0, tiled=True),
    )
    got_design = got_design.reshape(slot_count, panel_width)
    got_params = got_params.reshape(slot_count, param_count + 1)
    got_obs = got_params[:, param_count]
    got_params = got_params[:, :param_count]
    per_source = jnp.sum((epoch_table == device_index).astype(jnp.int32), axis=0)
    arc_start = jnp.sum((arc_ids < device_index).astype(jnp.int32))
    first_pos = jnp.mod(jnp.arange(tile_count, dtype=jnp.int32) - arc_start, tile_count)
    offset_in = jnp.arange(capacity, dtype=jnp.int32)
    order_pos = (first_pos[:, None] + offset_in[None, :] * tile_count).reshape(slot_count)
    usable = (offset_in[None, :] < per_source[:, None]).reshape(slot_count)
    position = jnp.arange(slot_count, dtype=jnp.int32)
    arc_length = jnp.sum(per_source)
    whitener = whiten_matrix(
        position, order_pos, position < arc_length, usable,
        autoreg[device_index], movavg[device_index],
    )
    design_bf, terms_bf, right_part = eliminate(whitener, got_design, got_params, got_obs, scale)
    swap = [(0, 1), (1, 0)]
    right_hand = lax.psum(right_part + lax.ppermute(right_part, "core", swap), "tmc")
    short_most = 5 * rows_dev // 8
    keep = (slot_count + short_most) // 2
    moved = lax.ppermute(design_bf[keep:], "core", swap)
    packed = design_bf[:keep].at[short_most : short_most + moved.shape[0]].add(moved)
    own_rows = jnp.concatenate([packed, terms_bf], axis=0)
    signed_rows = jnp.concatenate([packed, -terms_bf], axis=0)
    gathered = lax.all_gather(signed_rows, "panel", axis=1, tiled=True)
    gathered, right_hand = lax.optimization_barrier((gathered, right_hand))
    half = panel_width // core_count
    got_rows = lax.ppermute(gathered, "core", swap)
    got_cols = lax.ppermute(own_rows, "core", swap)
    row_side = jnp.concatenate([gathered, got_rows], axis=0)
    col_side = lax.dynamic_slice_in_dim(
        jnp.concatenate([own_rows, got_cols], axis=0), core_index * half, half, 1
    )
    product = lax.dot_general(
        row_side, col_side, (((0,), (0,)), ((), ())), preferred_element_type=jnp.float32
    )
    pair = lax.psum_scatter(
        (product * scale).astype(jnp.bfloat16), "tmc", scatter_dimension=0, tiled=True
    ).astype(jnp.float32)
    block_rows = pair.shape[0] // core_count
    by_core = pair.reshape(core_count, block_rows, half)
    mine = lax.dynamic_index_in_dim(by_core, core_index, 0, keepdims=False)
    given = lax.dynamic_index_in_dim(by_core, 1 - core_index, 0, keepdims=False)
    got = lax.ppermute(given, "core", swap)
    normal = jnp.where(
        core_index == 0,
        jnp.concatenate([mine, got], axis=1),
        jnp.concatenate([got, mine], axis=1),
    )
    return (normal, right_hand)


def solution(mesh):
    chips = mesh.devices.shape[0] // 2
    split = Mesh(
        mesh.devices.reshape(chips, 2, mesh.devices.shape[1]), ("tmc", "core", "panel")
    )
    in_specs = (P(TM, "panel"), P(TM, None), P(TM), P(), P(), P())
    out_specs = (P(TM, "panel"), P("panel"))
    return jax.shard_map(body, mesh=split, in_specs=in_specs, out_specs=out_specs, check_vma=False)
```

```python
import jax
import jax.numpy as jnp
from jax import lax
from jax.sharding import Mesh, PartitionSpec as P

TM = ("tmc", "core")


def whiten_matrix(order_row, order_col, usable_row, usable_col, ar_value, ma_value):
    spacing = order_row[:, None] - order_col[None, :]
    lag_steps = jnp.maximum(spacing - 1, 0)
    parity = (lag_steps % 2).astype(jnp.float32)
    flip_sign = 1.0 - 2.0 * parity
    decayed = (
        -(ar_value + ma_value)
        * flip_sign
        * jnp.exp(lag_steps.astype(jnp.float32) * jnp.log(ma_value))
    )
    entry = jnp.where(spacing == 0, jnp.float32(1.0), decayed)
    allowed = usable_row[:, None] & usable_col[None, :] & (spacing >= 0)
    return jnp.where(allowed, entry, jnp.float32(0.0)).astype(jnp.bfloat16)


def eliminate(whitener, rows_design, rows_params, rows_obs, scale):
    white_design = jnp.dot(whitener, rows_design, preferred_element_type=jnp.float32)
    white_params = jnp.dot(whitener, rows_params, preferred_element_type=jnp.float32)
    white_obs = jnp.dot(whitener, rows_obs, preferred_element_type=jnp.float32)
    param_count = rows_params.shape[1]
    param_gram = jnp.dot(white_params.T, white_params, precision=lax.Precision.HIGHEST) + jnp.eye(
        param_count, dtype=jnp.float32
    )
    factor = jnp.linalg.cholesky(param_gram)
    basis = lax.linalg.triangular_solve(factor, white_params.T, left_side=True, lower=True)
    arc_terms = jnp.dot(basis, white_design, precision=lax.Precision.HIGHEST)
    arc_rhs = jnp.dot(basis, white_obs, precision=lax.Precision.HIGHEST)
    right_part = (
        jnp.dot(white_design.T, white_obs, precision=lax.Precision.HIGHEST)
        - jnp.dot(arc_terms.T, arc_rhs, precision=lax.Precision.HIGHEST)
    ) * scale
    return (white_design.astype(jnp.bfloat16), basis, right_part)


def body(design, partials, observed, arc_of_row, autoreg, movavg):
    chip_count = lax.axis_size("tmc")
    core_count = lax.axis_size("core")
    core_index = lax.axis_index("core")
    tile_count = chip_count * core_count
    device_index = lax.axis_index("tmc") * core_count + core_index
    rows_dev = design.shape[0]
    panel_width = design.shape[1]
    param_count = partials.shape[1]
    capacity = 3 * rows_dev // 2 // tile_count
    slot_count = tile_count * capacity
    scale = 1.0 / (rows_dev * tile_count)
    arc_ids = arc_of_row[:, 0]
    epoch_table = arc_ids.reshape(rows_dev, tile_count)
    local_arcs = lax.dynamic_slice_in_dim(epoch_table, device_index, 1, 1)[:, 0]
    onehot = (local_arcs[:, None] == jnp.arange(tile_count, dtype=jnp.int32)[None, :]).astype(
        jnp.int32
    )
    earlier = jnp.cumsum(onehot, axis=0) - onehot
    within = jnp.sum(earlier * onehot, axis=1)
    target_slot = local_arcs * capacity + within
    source_row = (
        jnp.zeros((slot_count,), jnp.int32)
        .at[target_slot]
        .set(jnp.arange(1, rows_dev + 1, dtype=jnp.int32))
    )

    def pick_rows(values):
        padded = jnp.concatenate([jnp.zeros((1,) + values.shape[1:], values.dtype), values], axis=0)
        return jnp.take(padded, source_row, axis=0)

    send_design = pick_rows(design).reshape(tile_count, capacity, panel_width)
    with_obs = jnp.concatenate([partials, observed[:, None]], axis=1)
    send_params = pick_rows(with_obs).reshape(tile_count, capacity, param_count + 1)
    got_design, got_params = (
        lax.all_to_all(send_design, TM, split_axis=0, concat_axis=0, tiled=True),
        lax.all_to_all(send_params, TM, split_axis=0, concat_axis=0, tiled=True),
    )
    got_design = got_design.reshape(slot_count, panel_width)
    got_params = got_params.reshape(slot_count, param_count + 1)
    got_obs = got_params[:, param_count]
    got_params = got_params[:, :param_count]
    per_source = jnp.sum((epoch_table == device_index).astype(jnp.int32), axis=0)
    arc_start = jnp.sum((arc_ids < device_index).astype(jnp.int32))
    first_pos = jnp.mod(jnp.arange(tile_count, dtype=jnp.int32) - arc_start, tile_count)
    offset_in = jnp.arange(capacity, dtype=jnp.int32)
    order_pos = (first_pos[:, None] + offset_in[None, :] * tile_count).reshape(slot_count)
    usable = (offset_in[None, :] < per_source[:, None]).reshape(slot_count)
    position = jnp.arange(slot_count, dtype=jnp.int32)
    arc_length = jnp.sum(per_source)
    whitener = whiten_matrix(
        position, order_pos, position < arc_length, usable,
        autoreg[device_index], movavg[device_index],
    )
    design_bf, basis, right_part = eliminate(whitener, got_design, got_params, got_obs, scale)
    swap = [(0, 1), (1, 0)]
    right_hand = lax.psum(right_part + lax.ppermute(right_part, "core", swap), "tmc")
    short_most = 5 * rows_dev // 8
    keep = (slot_count + short_most) // 2
    moved = lax.ppermute(design_bf[keep:], "core", swap)
    packed = design_bf[:keep].at[short_most : short_most + moved.shape[0]].add(moved)
    gathered = lax.all_gather(packed, "panel", axis=1, tiled=True)
    gathered, right_hand = lax.optimization_barrier((gathered, right_hand))
    half = panel_width // core_count
    got_rows = lax.ppermute(gathered, "core", swap)
    got_basis = lax.ppermute(basis, "core", swap)
    moved_count = slot_count - keep

    def arc_terms(own_basis, home, away):
        upper = jnp.dot(own_basis[:, :keep], home.astype(jnp.float32), precision=lax.Precision.HIGHEST)
        lower = jnp.dot(
            own_basis[:, keep:],
            away[short_most : short_most + moved_count].astype(jnp.float32),
            precision=lax.Precision.HIGHEST,
        )
        return (upper + lower).astype(jnp.bfloat16)

    terms = jnp.concatenate(
        [arc_terms(basis, gathered, got_rows), arc_terms(got_basis, got_rows, gathered)], axis=0
    )
    design_side = jnp.concatenate([gathered, got_rows], axis=0)
    row_side = jnp.concatenate([design_side, -terms], axis=0)
    col_side = lax.dynamic_slice_in_dim(
        jnp.concatenate([design_side, terms], axis=0),
        lax.axis_index("panel") * panel_width + core_index * half, half, 1,
    )
    product = lax.dot_general(
        row_side, col_side, (((0,), (0,)), ((), ())), preferred_element_type=jnp.float32
    )
    pair = lax.psum_scatter(
        (product * scale).astype(jnp.bfloat16), "tmc", scatter_dimension=0, tiled=True
    ).astype(jnp.float32)
    block_rows = pair.shape[0] // core_count
    by_core = pair.reshape(core_count, block_rows, half)
    mine = lax.dynamic_index_in_dim(by_core, core_index, 0, keepdims=False)
    given = lax.dynamic_index_in_dim(by_core, 1 - core_index, 0, keepdims=False)
    got = lax.ppermute(given, "core", swap)
    normal = jnp.where(
        core_index == 0,
        jnp.concatenate([mine, got], axis=1),
        jnp.concatenate([got, mine], axis=1),
    )
    return (normal, right_hand)


def solution(mesh):
    chips = mesh.devices.shape[0] // 2
    split = Mesh(
        mesh.devices.reshape(chips, 2, mesh.devices.shape[1]), ("tmc", "core", "panel")
    )
    in_specs = (P(TM, "panel"), P(TM, None), P(TM), P(), P(), P())
    out_specs = (P(TM, "panel"), P("panel"))
    return jax.shard_map(body, mesh=split, in_specs=in_specs, out_specs=out_specs, check_vma=False)
```

```python
import jax
import jax.numpy as jnp
from jax import lax
from jax.sharding import Mesh, PartitionSpec as P

TM = ("tmc", "core")


def whiten_matrix(order_row, order_col, usable_row, usable_col, ar_value, ma_value):
    spacing = order_row[:, None] - order_col[None, :]
    lag_steps = jnp.maximum(spacing - 1, 0)
    parity = (lag_steps % 2).astype(jnp.float32)
    flip_sign = 1.0 - 2.0 * parity
    decayed = (
        -(ar_value + ma_value)
        * flip_sign
        * jnp.exp(lag_steps.astype(jnp.float32) * jnp.log(ma_value))
    )
    entry = jnp.where(spacing == 0, jnp.float32(1.0), decayed)
    allowed = usable_row[:, None] & usable_col[None, :] & (spacing >= 0)
    return jnp.where(allowed, entry, jnp.float32(0.0)).astype(jnp.bfloat16)


def eliminate(whitener, rows_design, rows_params, rows_obs, scale):
    white_design = jnp.dot(whitener, rows_design, preferred_element_type=jnp.float32)
    white_params = jnp.dot(whitener, rows_params, preferred_element_type=jnp.float32)
    white_obs = jnp.dot(whitener, rows_obs, preferred_element_type=jnp.float32)
    param_count = rows_params.shape[1]
    param_gram = jnp.dot(white_params.T, white_params, precision=lax.Precision.HIGHEST) + jnp.eye(
        param_count, dtype=jnp.float32
    )
    factor = jnp.linalg.cholesky(param_gram)
    basis = lax.linalg.triangular_solve(factor, white_params.T, left_side=True, lower=True)
    arc_terms = jnp.dot(basis, white_design, precision=lax.Precision.HIGHEST)
    arc_rhs = jnp.dot(basis, white_obs, precision=lax.Precision.HIGHEST)
    right_part = (
        jnp.dot(white_design.T, white_obs, precision=lax.Precision.HIGHEST)
        - jnp.dot(arc_terms.T, arc_rhs, precision=lax.Precision.HIGHEST)
    ) * scale
    return (white_design.astype(jnp.bfloat16), basis, right_part)


def body(design, partials, observed, arc_of_row, autoreg, movavg):
    chip_count = lax.axis_size("tmc")
    core_count = lax.axis_size("core")
    core_index = lax.axis_index("core")
    tile_count = chip_count * core_count
    device_index = lax.axis_index("tmc") * core_count + core_index
    rows_dev = design.shape[0]
    panel_width = design.shape[1]
    param_count = partials.shape[1]
    capacity = 3 * rows_dev // 2 // tile_count
    slot_count = tile_count * capacity
    scale = 1.0 / (rows_dev * tile_count)
    arc_ids = arc_of_row[:, 0]
    epoch_table = arc_ids.reshape(rows_dev, tile_count)
    local_arcs = lax.dynamic_slice_in_dim(epoch_table, device_index, 1, 1)[:, 0]
    onehot = (local_arcs[:, None] == jnp.arange(tile_count, dtype=jnp.int32)[None, :]).astype(
        jnp.int32
    )
    earlier = jnp.cumsum(onehot, axis=0) - onehot
    within = jnp.sum(earlier * onehot, axis=1)
    target_slot = local_arcs * capacity + within
    source_row = (
        jnp.zeros((slot_count,), jnp.int32)
        .at[target_slot]
        .set(jnp.arange(1, rows_dev + 1, dtype=jnp.int32))
    )

    def pick_rows(values):
        padded = jnp.concatenate([jnp.zeros((1,) + values.shape[1:], values.dtype), values], axis=0)
        return jnp.take(padded, source_row, axis=0)

    send_design = pick_rows(design).reshape(tile_count, capacity, panel_width)
    with_obs = jnp.concatenate([partials, observed[:, None]], axis=1)
    send_params = pick_rows(with_obs).reshape(tile_count, capacity, param_count + 1)
    got_params = lax.all_to_all(send_params, TM, split_axis=0, concat_axis=0, tiled=True)
    send_design, got_params = lax.optimization_barrier((send_design, got_params))
    got_design = lax.all_to_all(send_design, TM, split_axis=0, concat_axis=0, tiled=True)
    got_design = got_design.reshape(slot_count, panel_width)
    got_params = got_params.reshape(slot_count, param_count + 1)
    got_obs = got_params[:, param_count]
    got_params = got_params[:, :param_count]
    per_source = jnp.sum((epoch_table == device_index).astype(jnp.int32), axis=0)
    arc_start = jnp.sum((arc_ids < device_index).astype(jnp.int32))
    first_pos = jnp.mod(jnp.arange(tile_count, dtype=jnp.int32) - arc_start, tile_count)
    offset_in = jnp.arange(capacity, dtype=jnp.int32)
    order_pos = (first_pos[:, None] + offset_in[None, :] * tile_count).reshape(slot_count)
    usable = (offset_in[None, :] < per_source[:, None]).reshape(slot_count)
    position = jnp.arange(slot_count, dtype=jnp.int32)
    arc_length = jnp.sum(per_source)
    whitener = whiten_matrix(
        position, order_pos, position < arc_length, usable,
        autoreg[device_index], movavg[device_index],
    )
    design_bf, basis, right_part = eliminate(whitener, got_design, got_params, got_obs, scale)
    swap = [(0, 1), (1, 0)]
    right_hand = lax.psum(right_part + lax.ppermute(right_part, "core", swap), "tmc")
    short_most = 5 * rows_dev // 8
    keep = (slot_count + short_most) // 2
    moved = lax.ppermute(design_bf[keep:], "core", swap)
    packed = design_bf[:keep].at[short_most : short_most + moved.shape[0]].add(moved)
    gathered = lax.all_gather(packed, "panel", axis=1, tiled=True)
    gathered, right_hand = lax.optimization_barrier((gathered, right_hand))
    half = panel_width // core_count
    got_rows = lax.ppermute(gathered, "core", swap)
    got_basis = lax.ppermute(basis, "core", swap)
    moved_count = slot_count - keep

    def arc_terms(own_basis, home, away):
        own_basis = own_basis.astype(jnp.bfloat16)
        upper = jnp.dot(own_basis[:, :keep], home, preferred_element_type=jnp.float32)
        lower = jnp.dot(
            own_basis[:, keep:],
            away[short_most : short_most + moved_count],
            preferred_element_type=jnp.float32,
        )
        return (upper + lower).astype(jnp.bfloat16)

    terms = jnp.concatenate(
        [arc_terms(basis, gathered, got_rows), arc_terms(got_basis, got_rows, gathered)], axis=0
    )
    design_side = jnp.concatenate([gathered, got_rows], axis=0)
    row_side = jnp.concatenate([design_side, -terms], axis=0)
    col_side = lax.dynamic_slice_in_dim(
        jnp.concatenate([design_side, terms], axis=0),
        lax.axis_index("panel") * panel_width + core_index * half, half, 1,
    )
    product = lax.dot_general(
        row_side, col_side, (((0,), (0,)), ((), ())), preferred_element_type=jnp.float32
    )
    pair = lax.psum_scatter(
        (product * scale).astype(jnp.bfloat16), "tmc", scatter_dimension=0, tiled=True
    ).astype(jnp.float32)
    block_rows = pair.shape[0] // core_count
    by_core = pair.reshape(core_count, block_rows, half)
    mine = lax.dynamic_index_in_dim(by_core, core_index, 0, keepdims=False)
    given = lax.dynamic_index_in_dim(by_core, 1 - core_index, 0, keepdims=False)
    got = lax.ppermute(given, "core", swap)
    normal = jnp.where(
        core_index == 0,
        jnp.concatenate([mine, got], axis=1),
        jnp.concatenate([got, mine], axis=1),
    )
    return (normal, right_hand)


def solution(mesh):
    chips = mesh.devices.shape[0] // 2
    split = Mesh(
        mesh.devices.reshape(chips, 2, mesh.devices.shape[1]), ("tmc", "core", "panel")
    )
    in_specs = (P(TM, "panel"), P(TM, None), P(TM), P(), P(), P())
    out_specs = (P(TM, "panel"), P("panel"))
    return jax.shard_map(body, mesh=split, in_specs=in_specs, out_specs=out_specs, check_vma=False)
```

```python
import jax
import jax.numpy as jnp
from jax import lax
from jax.sharding import Mesh, PartitionSpec as P

TM = ("tmc", "core")


def whiten_matrix(order_row, order_col, usable_row, usable_col, ar_value, ma_value):
    spacing = order_row[:, None] - order_col[None, :]
    lag_steps = jnp.maximum(spacing - 1, 0)
    parity = (lag_steps % 2).astype(jnp.float32)
    flip_sign = 1.0 - 2.0 * parity
    decayed = (
        -(ar_value + ma_value)
        * flip_sign
        * jnp.exp(lag_steps.astype(jnp.float32) * jnp.log(ma_value))
    )
    entry = jnp.where(spacing == 0, jnp.float32(1.0), decayed)
    allowed = usable_row[:, None] & usable_col[None, :] & (spacing >= 0)
    return jnp.where(allowed, entry, jnp.float32(0.0)).astype(jnp.bfloat16)


def eliminate(whitener, rows_design, rows_params, rows_obs, scale):
    white_design = jnp.dot(whitener, rows_design, preferred_element_type=jnp.float32)
    white_params = jnp.dot(whitener, rows_params, preferred_element_type=jnp.float32)
    white_obs = jnp.dot(whitener, rows_obs, preferred_element_type=jnp.float32)
    param_count = rows_params.shape[1]
    param_gram = jnp.dot(white_params.T, white_params, precision=lax.Precision.HIGHEST) + jnp.eye(
        param_count, dtype=jnp.float32
    )
    factor = jnp.linalg.cholesky(param_gram)
    basis = lax.linalg.triangular_solve(factor, white_params.T, left_side=True, lower=True)
    arc_terms = jnp.dot(basis, white_design, precision=lax.Precision.HIGHEST)
    arc_rhs = jnp.dot(basis, white_obs, precision=lax.Precision.HIGHEST)
    right_part = (
        jnp.dot(white_design.T, white_obs, precision=lax.Precision.HIGHEST)
        - jnp.dot(arc_terms.T, arc_rhs, precision=lax.Precision.HIGHEST)
    ) * scale
    return (white_design.astype(jnp.bfloat16), basis, right_part)


def body(design, partials, observed, arc_of_row, autoreg, movavg):
    chip_count = lax.axis_size("tmc")
    core_count = lax.axis_size("core")
    core_index = lax.axis_index("core")
    tile_count = chip_count * core_count
    device_index = lax.axis_index("tmc") * core_count + core_index
    rows_dev = design.shape[0]
    panel_width = design.shape[1]
    param_count = partials.shape[1]
    capacity = 3 * rows_dev // 2 // tile_count
    slot_count = tile_count * capacity
    scale = 1.0 / (rows_dev * tile_count)
    arc_ids = arc_of_row[:, 0]
    epoch_table = arc_ids.reshape(rows_dev, tile_count)
    local_arcs = lax.dynamic_slice_in_dim(epoch_table, device_index, 1, 1)[:, 0]
    onehot = (local_arcs[:, None] == jnp.arange(tile_count, dtype=jnp.int32)[None, :]).astype(
        jnp.int32
    )
    earlier = jnp.cumsum(onehot, axis=0) - onehot
    within = jnp.sum(earlier * onehot, axis=1)
    target_slot = local_arcs * capacity + within
    source_row = (
        jnp.zeros((slot_count,), jnp.int32)
        .at[target_slot]
        .set(jnp.arange(1, rows_dev + 1, dtype=jnp.int32))
    )

    def pick_rows(values):
        padded = jnp.concatenate([jnp.zeros((1,) + values.shape[1:], values.dtype), values], axis=0)
        return jnp.take(padded, source_row, axis=0)

    send_design = pick_rows(design).reshape(tile_count, capacity, panel_width)
    with_obs = jnp.concatenate([partials, observed[:, None]], axis=1)
    send_params = pick_rows(with_obs).reshape(tile_count, capacity, param_count + 1)
    got_params = lax.all_to_all(send_params, TM, split_axis=0, concat_axis=0, tiled=True)
    send_design, got_params = lax.optimization_barrier((send_design, got_params))
    got_design = lax.all_to_all(send_design, TM, split_axis=0, concat_axis=0, tiled=True)
    got_design = got_design.reshape(slot_count, panel_width)
    got_params = got_params.reshape(slot_count, param_count + 1)
    got_obs = got_params[:, param_count]
    got_params = got_params[:, :param_count]
    per_source = jnp.sum((epoch_table == device_index).astype(jnp.int32), axis=0)
    arc_start = jnp.sum((arc_ids < device_index).astype(jnp.int32))
    first_pos = jnp.mod(jnp.arange(tile_count, dtype=jnp.int32) - arc_start, tile_count)
    offset_in = jnp.arange(capacity, dtype=jnp.int32)
    order_pos = (first_pos[:, None] + offset_in[None, :] * tile_count).reshape(slot_count)
    usable = (offset_in[None, :] < per_source[:, None]).reshape(slot_count)
    position = jnp.arange(slot_count, dtype=jnp.int32)
    arc_length = jnp.sum(per_source)
    whitener = whiten_matrix(
        position, order_pos, position < arc_length, usable,
        autoreg[device_index], movavg[device_index],
    )
    design_bf, basis, right_part = eliminate(whitener, got_design, got_params, got_obs, scale)
    swap = [(0, 1), (1, 0)]
    short_most = 5 * rows_dev // 8
    keep = (slot_count + short_most) // 2
    moved = lax.ppermute(design_bf[keep:], "core", swap)
    packed = design_bf[:keep].at[short_most : short_most + moved.shape[0]].add(moved)
    packed, right_part = lax.optimization_barrier((packed, right_part))
    gathered = lax.all_gather(packed, "panel", axis=1, tiled=True)
    right_hand = lax.psum(right_part + lax.ppermute(right_part, "core", swap), "tmc")
    gathered, right_hand = lax.optimization_barrier((gathered, right_hand))
    half = panel_width // core_count
    got_rows = lax.ppermute(gathered, "core", swap)
    got_basis = lax.ppermute(basis, "core", swap)
    moved_count = slot_count - keep

    def spread(own_basis):
        lead = own_basis[:, :keep]
        tail = jnp.pad(own_basis[:, keep:], ((0, 0), (short_most, keep - short_most - moved_count)))
        return lead, tail

    own_lead, own_tail = spread(basis)
    far_lead, far_tail = spread(got_basis)
    stacked_basis = jnp.concatenate(
        [
            jnp.concatenate([own_lead, own_tail], axis=1),
            jnp.concatenate([far_tail, far_lead], axis=1),
        ],
        axis=0,
    ).astype(jnp.bfloat16)
    design_side = jnp.concatenate([gathered, got_rows], axis=0)
    terms = jnp.dot(stacked_basis, design_side, preferred_element_type=jnp.float32).astype(
        jnp.bfloat16
    )
    row_side = jnp.concatenate([design_side, -terms], axis=0)
    col_side = lax.dynamic_slice_in_dim(
        jnp.concatenate([design_side, terms], axis=0),
        lax.axis_index("panel") * panel_width + core_index * half, half, 1,
    )
    product = lax.dot_general(
        row_side, col_side, (((0,), (0,)), ((), ())), preferred_element_type=jnp.float32
    )
    pair = lax.psum_scatter(
        (product * scale).astype(jnp.bfloat16), "tmc", scatter_dimension=0, tiled=True
    ).astype(jnp.float32)
    block_rows = pair.shape[0] // core_count
    by_core = pair.reshape(core_count, block_rows, half)
    mine = lax.dynamic_index_in_dim(by_core, core_index, 0, keepdims=False)
    given = lax.dynamic_index_in_dim(by_core, 1 - core_index, 0, keepdims=False)
    got = lax.ppermute(given, "core", swap)
    normal = jnp.where(
        core_index == 0,
        jnp.concatenate([mine, got], axis=1),
        jnp.concatenate([got, mine], axis=1),
    )
    return (normal, right_hand)


def solution(mesh):
    chips = mesh.devices.shape[0] // 2
    split = Mesh(
        mesh.devices.reshape(chips, 2, mesh.devices.shape[1]), ("tmc", "core", "panel")
    )
    in_specs = (P(TM, "panel"), P(TM, None), P(TM), P(), P(), P())
    out_specs = (P(TM, "panel"), P("panel"))
    return jax.shard_map(body, mesh=split, in_specs=in_specs, out_specs=out_specs, check_vma=False)
```

```python
import jax
import jax.numpy as jnp
from jax import lax
from jax.sharding import Mesh, PartitionSpec as P

TM = ("tmc", "core")


def whiten_matrix(order_row, order_col, usable_row, usable_col, ar_value, ma_value):
    spacing = order_row[:, None] - order_col[None, :]
    lag_steps = jnp.maximum(spacing - 1, 0)
    parity = (lag_steps % 2).astype(jnp.float32)
    flip_sign = 1.0 - 2.0 * parity
    decayed = (
        -(ar_value + ma_value)
        * flip_sign
        * jnp.exp(lag_steps.astype(jnp.float32) * jnp.log(ma_value))
    )
    entry = jnp.where(spacing == 0, jnp.float32(1.0), decayed)
    allowed = usable_row[:, None] & usable_col[None, :] & (spacing >= 0)
    return jnp.where(allowed, entry, jnp.float32(0.0)).astype(jnp.bfloat16)


def eliminate(whitener, rows_design, rows_params, rows_obs, scale):
    white_design = jnp.dot(whitener, rows_design, preferred_element_type=jnp.float32)
    white_params = jnp.dot(whitener, rows_params, preferred_element_type=jnp.float32)
    white_obs = jnp.dot(whitener, rows_obs, preferred_element_type=jnp.float32)
    param_count = rows_params.shape[1]
    param_gram = jnp.dot(white_params.T, white_params, precision=lax.Precision.HIGHEST) + jnp.eye(
        param_count, dtype=jnp.float32
    )
    factor = jnp.linalg.cholesky(param_gram)
    basis = lax.linalg.triangular_solve(factor, white_params.T, left_side=True, lower=True)
    arc_terms = jnp.dot(basis, white_design, precision=lax.Precision.HIGHEST)
    arc_rhs = jnp.dot(basis, white_obs, precision=lax.Precision.HIGHEST)
    right_part = (
        jnp.dot(white_design.T, white_obs, precision=lax.Precision.HIGHEST)
        - jnp.dot(arc_terms.T, arc_rhs, precision=lax.Precision.HIGHEST)
    ) * scale
    return (white_design.astype(jnp.bfloat16), basis, right_part)


def body(design, partials, observed, arc_of_row, autoreg, movavg):
    chip_count = lax.axis_size("tmc")
    core_count = lax.axis_size("core")
    core_index = lax.axis_index("core")
    tile_count = chip_count * core_count
    device_index = lax.axis_index("tmc") * core_count + core_index
    rows_dev = design.shape[0]
    panel_width = design.shape[1]
    param_count = partials.shape[1]
    capacity = 3 * rows_dev // 2 // tile_count
    slot_count = tile_count * capacity
    scale = 1.0 / (rows_dev * tile_count)
    arc_ids = arc_of_row[:, 0]
    epoch_table = arc_ids.reshape(rows_dev, tile_count)
    local_arcs = lax.dynamic_slice_in_dim(epoch_table, device_index, 1, 1)[:, 0]
    onehot = (local_arcs[:, None] == jnp.arange(tile_count, dtype=jnp.int32)[None, :]).astype(
        jnp.int32
    )
    earlier = jnp.cumsum(onehot, axis=0) - onehot
    within = jnp.sum(earlier * onehot, axis=1)
    target_slot = local_arcs * capacity + within
    source_row = (
        jnp.zeros((slot_count,), jnp.int32)
        .at[target_slot]
        .set(jnp.arange(1, rows_dev + 1, dtype=jnp.int32))
    )

    def pick_rows(values):
        padded = jnp.concatenate([jnp.zeros((1,) + values.shape[1:], values.dtype), values], axis=0)
        return jnp.take(padded, source_row, axis=0)

    send_design = pick_rows(design).reshape(tile_count, capacity, panel_width)
    with_obs = jnp.concatenate([partials, observed[:, None]], axis=1)
    send_params = pick_rows(with_obs).reshape(tile_count, capacity, param_count + 1)
    got_params = lax.all_to_all(send_params, TM, split_axis=0, concat_axis=0, tiled=True)
    send_design, got_params = lax.optimization_barrier((send_design, got_params))
    got_design = lax.all_to_all(send_design, TM, split_axis=0, concat_axis=0, tiled=True)
    got_design = got_design.reshape(slot_count, panel_width)
    got_params = got_params.reshape(slot_count, param_count + 1)
    got_obs = got_params[:, param_count]
    got_params = got_params[:, :param_count]
    per_source = jnp.sum((epoch_table == device_index).astype(jnp.int32), axis=0)
    arc_start = jnp.sum((arc_ids < device_index).astype(jnp.int32))
    first_pos = jnp.mod(jnp.arange(tile_count, dtype=jnp.int32) - arc_start, tile_count)
    offset_in = jnp.arange(capacity, dtype=jnp.int32)
    order_pos = (first_pos[:, None] + offset_in[None, :] * tile_count).reshape(slot_count)
    usable = (offset_in[None, :] < per_source[:, None]).reshape(slot_count)
    position = jnp.arange(slot_count, dtype=jnp.int32)
    arc_length = jnp.sum(per_source)
    whitener = whiten_matrix(
        position, order_pos, position < arc_length, usable,
        autoreg[device_index], movavg[device_index],
    )
    design_bf, basis, right_part = eliminate(whitener, got_design, got_params, got_obs, scale)
    swap = [(0, 1), (1, 0)]
    short_most = 5 * rows_dev // 8
    keep = (slot_count + short_most) // 2
    moved = lax.ppermute(design_bf[keep:], "core", swap)
    packed = design_bf[:keep].at[short_most : short_most + moved.shape[0]].add(moved)
    got_basis = lax.ppermute(basis, "core", swap)
    packed, right_part, got_basis = lax.optimization_barrier((packed, right_part, got_basis))
    gathered = lax.all_gather(packed, "panel", axis=1, tiled=True)
    right_hand = lax.psum(right_part + lax.ppermute(right_part, "core", swap), "tmc")
    gathered, right_hand = lax.optimization_barrier((gathered, right_hand))
    half = panel_width // core_count
    got_rows = lax.ppermute(gathered, "core", swap)
    moved_count = slot_count - keep

    def spread(own_basis):
        lead = own_basis[:, :keep]
        tail = jnp.pad(own_basis[:, keep:], ((0, 0), (short_most, keep - short_most - moved_count)))
        return lead, tail

    own_lead, own_tail = spread(basis)
    far_lead, far_tail = spread(got_basis)
    stacked_basis = jnp.concatenate(
        [
            jnp.concatenate([own_lead, own_tail], axis=1),
            jnp.concatenate([far_tail, far_lead], axis=1),
        ],
        axis=0,
    ).astype(jnp.bfloat16)
    design_side = jnp.concatenate([gathered, got_rows], axis=0)
    terms = jnp.dot(stacked_basis, design_side, preferred_element_type=jnp.float32).astype(
        jnp.bfloat16
    )
    row_side = jnp.concatenate([design_side, -terms], axis=0)
    col_side = lax.dynamic_slice_in_dim(
        jnp.concatenate([design_side, terms], axis=0),
        lax.axis_index("panel") * panel_width + core_index * half, half, 1,
    )
    product = lax.dot_general(
        row_side, col_side, (((0,), (0,)), ((), ())), preferred_element_type=jnp.float32
    )
    pair = lax.psum_scatter(
        (product * scale).astype(jnp.bfloat16), "tmc", scatter_dimension=0, tiled=True
    ).astype(jnp.float32)
    block_rows = pair.shape[0] // core_count
    by_core = pair.reshape(core_count, block_rows, half)
    mine = lax.dynamic_index_in_dim(by_core, core_index, 0, keepdims=False)
    given = lax.dynamic_index_in_dim(by_core, 1 - core_index, 0, keepdims=False)
    got = lax.ppermute(given, "core", swap)
    normal = jnp.where(
        core_index == 0,
        jnp.concatenate([mine, got], axis=1),
        jnp.concatenate([got, mine], axis=1),
    )
    return (normal, right_hand)


def solution(mesh):
    chips = mesh.devices.shape[0] // 2
    split = Mesh(
        mesh.devices.reshape(chips, 2, mesh.devices.shape[1]), ("tmc", "core", "panel")
    )
    in_specs = (P(TM, "panel"), P(TM, None), P(TM), P(), P(), P())
    out_specs = (P(TM, "panel"), P("panel"))
    return jax.shard_map(body, mesh=split, in_specs=in_specs, out_specs=out_specs, check_vma=False)
```

```python
import jax
import jax.numpy as jnp
from jax import lax
from jax.sharding import Mesh, PartitionSpec as P

TM = ("tmc", "core")


def whiten_matrix(order_row, order_col, usable_row, usable_col, ar_value, ma_value):
    spacing = order_row[:, None] - order_col[None, :]
    lag_steps = jnp.maximum(spacing - 1, 0)
    parity = (lag_steps % 2).astype(jnp.float32)
    flip_sign = 1.0 - 2.0 * parity
    decayed = (
        -(ar_value + ma_value)
        * flip_sign
        * jnp.exp(lag_steps.astype(jnp.float32) * jnp.log(ma_value))
    )
    entry = jnp.where(spacing == 0, jnp.float32(1.0), decayed)
    allowed = usable_row[:, None] & usable_col[None, :] & (spacing >= 0)
    return jnp.where(allowed, entry, jnp.float32(0.0)).astype(jnp.bfloat16)


def eliminate(whitener, rows_design, rows_params, rows_obs, scale):
    white_design = jnp.dot(whitener, rows_design, preferred_element_type=jnp.float32)
    white_params = jnp.dot(whitener, rows_params, preferred_element_type=jnp.float32)
    white_obs = jnp.dot(whitener, rows_obs, preferred_element_type=jnp.float32)
    param_count = rows_params.shape[1]
    param_gram = jnp.dot(white_params.T, white_params, precision=lax.Precision.HIGHEST) + jnp.eye(
        param_count, dtype=jnp.float32
    )
    factor = jnp.linalg.cholesky(param_gram)
    basis = lax.linalg.triangular_solve(factor, white_params.T, left_side=True, lower=True)
    arc_terms = jnp.dot(basis, white_design, precision=lax.Precision.HIGHEST)
    arc_rhs = jnp.dot(basis, white_obs, precision=lax.Precision.HIGHEST)
    right_part = (
        jnp.dot(white_design.T, white_obs, precision=lax.Precision.HIGHEST)
        - jnp.dot(arc_terms.T, arc_rhs, precision=lax.Precision.HIGHEST)
    ) * scale
    return (white_design.astype(jnp.bfloat16), basis, right_part)


def body(design, partials, observed, arc_of_row, autoreg, movavg):
    chip_count = lax.axis_size("tmc")
    core_count = lax.axis_size("core")
    core_index = lax.axis_index("core")
    tile_count = chip_count * core_count
    device_index = lax.axis_index("tmc") * core_count + core_index
    rows_dev = design.shape[0]
    panel_width = design.shape[1]
    param_count = partials.shape[1]
    capacity = 3 * rows_dev // 2 // tile_count
    slot_count = tile_count * capacity
    scale = 1.0 / (rows_dev * tile_count)
    arc_ids = arc_of_row[:, 0]
    epoch_table = arc_ids.reshape(rows_dev, tile_count)
    local_arcs = lax.dynamic_slice_in_dim(epoch_table, device_index, 1, 1)[:, 0]
    onehot = (local_arcs[:, None] == jnp.arange(tile_count, dtype=jnp.int32)[None, :]).astype(
        jnp.int32
    )
    earlier = jnp.cumsum(onehot, axis=0) - onehot
    within = jnp.sum(earlier * onehot, axis=1)
    target_slot = local_arcs * capacity + within
    chooser = (
        target_slot[None, :] == jnp.arange(slot_count, dtype=jnp.int32)[:, None]
    ).astype(jnp.bfloat16)

    def pick_rows(values):
        picked = jnp.dot(chooser, values, preferred_element_type=jnp.float32)
        return picked.astype(values.dtype)

    send_design = pick_rows(design).reshape(tile_count, capacity, panel_width)
    with_obs = jnp.concatenate([partials, observed[:, None]], axis=1)
    send_params = pick_rows(with_obs).reshape(tile_count, capacity, param_count + 1)
    got_params = lax.all_to_all(send_params, TM, split_axis=0, concat_axis=0, tiled=True)
    send_design, got_params = lax.optimization_barrier((send_design, got_params))
    got_design = lax.all_to_all(send_design, TM, split_axis=0, concat_axis=0, tiled=True)
    got_design = got_design.reshape(slot_count, panel_width)
    got_params = got_params.reshape(slot_count, param_count + 1)
    got_obs = got_params[:, param_count]
    got_params = got_params[:, :param_count]
    per_source = jnp.sum((epoch_table == device_index).astype(jnp.int32), axis=0)
    arc_start = jnp.sum((arc_ids < device_index).astype(jnp.int32))
    first_pos = jnp.mod(jnp.arange(tile_count, dtype=jnp.int32) - arc_start, tile_count)
    offset_in = jnp.arange(capacity, dtype=jnp.int32)
    order_pos = (first_pos[:, None] + offset_in[None, :] * tile_count).reshape(slot_count)
    usable = (offset_in[None, :] < per_source[:, None]).reshape(slot_count)
    position = jnp.arange(slot_count, dtype=jnp.int32)
    arc_length = jnp.sum(per_source)
    whitener = whiten_matrix(
        position, order_pos, position < arc_length, usable,
        autoreg[device_index], movavg[device_index],
    )
    design_bf, basis, right_part = eliminate(whitener, got_design, got_params, got_obs, scale)
    swap = [(0, 1), (1, 0)]
    short_most = 5 * rows_dev // 8
    keep = (slot_count + short_most) // 2
    moved = lax.ppermute(design_bf[keep:], "core", swap)
    packed = design_bf[:keep].at[short_most : short_most + moved.shape[0]].add(moved)
    got_basis = lax.ppermute(basis, "core", swap)
    packed, right_part, got_basis = lax.optimization_barrier((packed, right_part, got_basis))
    gathered = lax.all_gather(packed, "panel", axis=1, tiled=True)
    right_hand = lax.psum(right_part + lax.ppermute(right_part, "core", swap), "tmc")
    gathered, right_hand = lax.optimization_barrier((gathered, right_hand))
    half = panel_width // core_count
    got_rows = lax.ppermute(gathered, "core", swap)
    moved_count = slot_count - keep

    def spread(own_basis):
        lead = own_basis[:, :keep]
        tail = jnp.pad(own_basis[:, keep:], ((0, 0), (short_most, keep - short_most - moved_count)))
        return lead, tail

    own_lead, own_tail = spread(basis)
    far_lead, far_tail = spread(got_basis)
    stacked_basis = jnp.concatenate(
        [
            jnp.concatenate([own_lead, own_tail], axis=1),
            jnp.concatenate([far_tail, far_lead], axis=1),
        ],
        axis=0,
    ).astype(jnp.bfloat16)
    design_side = jnp.concatenate([gathered, got_rows], axis=0)
    terms = jnp.dot(stacked_basis, design_side, preferred_element_type=jnp.float32).astype(
        jnp.bfloat16
    )
    row_side = jnp.concatenate([design_side, -terms], axis=0)
    col_side = lax.dynamic_slice_in_dim(
        jnp.concatenate([design_side, terms], axis=0),
        lax.axis_index("panel") * panel_width + core_index * half, half, 1,
    )
    product = lax.dot_general(
        row_side, col_side, (((0,), (0,)), ((), ())), preferred_element_type=jnp.float32
    )
    pair = lax.psum_scatter(
        (product * scale).astype(jnp.bfloat16), "tmc", scatter_dimension=0, tiled=True
    ).astype(jnp.float32)
    block_rows = pair.shape[0] // core_count
    by_core = pair.reshape(core_count, block_rows, half)
    mine = lax.dynamic_index_in_dim(by_core, core_index, 0, keepdims=False)
    given = lax.dynamic_index_in_dim(by_core, 1 - core_index, 0, keepdims=False)
    got = lax.ppermute(given, "core", swap)
    normal = jnp.where(
        core_index == 0,
        jnp.concatenate([mine, got], axis=1),
        jnp.concatenate([got, mine], axis=1),
    )
    return (normal, right_hand)


def solution(mesh):
    chips = mesh.devices.shape[0] // 2
    split = Mesh(
        mesh.devices.reshape(chips, 2, mesh.devices.shape[1]), ("tmc", "core", "panel")
    )
    in_specs = (P(TM, "panel"), P(TM, None), P(TM), P(), P(), P())
    out_specs = (P(TM, "panel"), P("panel"))
    return jax.shard_map(body, mesh=split, in_specs=in_specs, out_specs=out_specs, check_vma=False)
```

```python
import jax
import jax.numpy as jnp
from jax import lax
from jax.sharding import Mesh, PartitionSpec as P

TM = ("tmc", "core")


def whiten_matrix(order_row, order_col, usable_row, usable_col, ar_value, ma_value):
    spacing = order_row[:, None] - order_col[None, :]
    lag_steps = jnp.maximum(spacing - 1, 0)
    parity = (lag_steps % 2).astype(jnp.float32)
    flip_sign = 1.0 - 2.0 * parity
    decayed = (
        -(ar_value + ma_value)
        * flip_sign
        * jnp.exp(lag_steps.astype(jnp.float32) * jnp.log(ma_value))
    )
    entry = jnp.where(spacing == 0, jnp.float32(1.0), decayed)
    allowed = usable_row[:, None] & usable_col[None, :] & (spacing >= 0)
    return jnp.where(allowed, entry, jnp.float32(0.0)).astype(jnp.bfloat16)


def eliminate(whitener, rows_design, rows_params, rows_obs, scale):
    white_design = jnp.dot(whitener, rows_design, preferred_element_type=jnp.float32)
    white_params = jnp.dot(whitener, rows_params, preferred_element_type=jnp.float32)
    white_obs = jnp.dot(whitener, rows_obs, preferred_element_type=jnp.float32)
    param_count = rows_params.shape[1]
    param_gram = jnp.dot(white_params.T, white_params, precision=lax.Precision.HIGHEST) + jnp.eye(
        param_count, dtype=jnp.float32
    )
    factor = jnp.linalg.cholesky(param_gram)
    basis = lax.linalg.triangular_solve(factor, white_params.T, left_side=True, lower=True)
    arc_terms = jnp.dot(basis, white_design, precision=lax.Precision.HIGHEST)
    arc_rhs = jnp.dot(basis, white_obs, precision=lax.Precision.HIGHEST)
    right_part = (
        jnp.dot(white_design.T, white_obs, precision=lax.Precision.HIGHEST)
        - jnp.dot(arc_terms.T, arc_rhs, precision=lax.Precision.HIGHEST)
    ) * scale
    return (white_design.astype(jnp.bfloat16), basis, right_part)


def body(design, partials, observed, arc_of_row, autoreg, movavg):
    chip_count = lax.axis_size("tmc")
    core_count = lax.axis_size("core")
    core_index = lax.axis_index("core")
    tile_count = chip_count * core_count
    device_index = lax.axis_index("tmc") * core_count + core_index
    rows_dev = design.shape[0]
    panel_width = design.shape[1]
    param_count = partials.shape[1]
    capacity = 3 * rows_dev // 2 // tile_count
    slot_count = tile_count * capacity
    scale = 1.0 / (rows_dev * tile_count)
    arc_ids = arc_of_row[:, 0]
    epoch_table = arc_ids.reshape(rows_dev, tile_count)
    local_arcs = lax.dynamic_slice_in_dim(epoch_table, device_index, 1, 1)[:, 0]
    onehot = (local_arcs[:, None] == jnp.arange(tile_count, dtype=jnp.int32)[None, :]).astype(
        jnp.int32
    )
    earlier = jnp.cumsum(onehot, axis=0) - onehot
    within = jnp.sum(earlier * onehot, axis=1)
    target_slot = local_arcs * capacity + within
    chooser = (
        target_slot[None, :] == jnp.arange(slot_count, dtype=jnp.int32)[:, None]
    ).astype(jnp.bfloat16)

    def pick_rows(values):
        picked = jnp.dot(chooser, values, preferred_element_type=jnp.float32)
        return picked.astype(values.dtype)

    bundle = jnp.concatenate([design, partials, observed[:, None]], axis=1)
    sent = pick_rows(bundle).reshape(tile_count, capacity, bundle.shape[1])
    got = lax.all_to_all(sent, TM, split_axis=0, concat_axis=0, tiled=True)
    got = got.reshape(slot_count, bundle.shape[1])
    got_design = got[:, :panel_width]
    got_params = got[:, panel_width : panel_width + param_count]
    got_obs = got[:, panel_width + param_count]
    per_source = jnp.sum((epoch_table == device_index).astype(jnp.int32), axis=0)
    arc_start = jnp.sum((arc_ids < device_index).astype(jnp.int32))
    first_pos = jnp.mod(jnp.arange(tile_count, dtype=jnp.int32) - arc_start, tile_count)
    offset_in = jnp.arange(capacity, dtype=jnp.int32)
    order_pos = (first_pos[:, None] + offset_in[None, :] * tile_count).reshape(slot_count)
    usable = (offset_in[None, :] < per_source[:, None]).reshape(slot_count)
    position = jnp.arange(slot_count, dtype=jnp.int32)
    arc_length = jnp.sum(per_source)
    whitener = whiten_matrix(
        position, order_pos, position < arc_length, usable,
        autoreg[device_index], movavg[device_index],
    )
    design_bf, basis, right_part = eliminate(whitener, got_design, got_params, got_obs, scale)
    swap = [(0, 1), (1, 0)]
    short_most = 5 * rows_dev // 8
    keep = (slot_count + short_most) // 2
    moved = lax.ppermute(design_bf[keep:], "core", swap)
    packed = design_bf[:keep].at[short_most : short_most + moved.shape[0]].add(moved)
    got_basis = lax.ppermute(basis, "core", swap)
    packed, right_part, got_basis = lax.optimization_barrier((packed, right_part, got_basis))
    gathered = lax.all_gather(packed, "panel", axis=1, tiled=True)
    right_hand = lax.psum(right_part + lax.ppermute(right_part, "core", swap), "tmc")
    gathered, right_hand = lax.optimization_barrier((gathered, right_hand))
    half = panel_width // core_count
    got_rows = lax.ppermute(gathered, "core", swap)
    moved_count = slot_count - keep

    def spread(own_basis):
        lead = own_basis[:, :keep]
        tail = jnp.pad(own_basis[:, keep:], ((0, 0), (short_most, keep - short_most - moved_count)))
        return lead, tail

    own_lead, own_tail = spread(basis)
    far_lead, far_tail = spread(got_basis)
    stacked_basis = jnp.concatenate(
        [
            jnp.concatenate([own_lead, own_tail], axis=1),
            jnp.concatenate([far_tail, far_lead], axis=1),
        ],
        axis=0,
    ).astype(jnp.bfloat16)
    design_side = jnp.concatenate([gathered, got_rows], axis=0)
    terms = jnp.dot(stacked_basis, design_side, preferred_element_type=jnp.float32).astype(
        jnp.bfloat16
    )
    row_side = jnp.concatenate([design_side, -terms], axis=0)
    col_side = lax.dynamic_slice_in_dim(
        jnp.concatenate([design_side, terms], axis=0),
        lax.axis_index("panel") * panel_width + core_index * half, half, 1,
    )
    product = lax.dot_general(
        row_side, col_side, (((0,), (0,)), ((), ())), preferred_element_type=jnp.float32
    )
    pair = lax.psum_scatter(
        (product * scale).astype(jnp.bfloat16), "tmc", scatter_dimension=0, tiled=True
    ).astype(jnp.float32)
    block_rows = pair.shape[0] // core_count
    by_core = pair.reshape(core_count, block_rows, half)
    mine = lax.dynamic_index_in_dim(by_core, core_index, 0, keepdims=False)
    given = lax.dynamic_index_in_dim(by_core, 1 - core_index, 0, keepdims=False)
    got = lax.ppermute(given, "core", swap)
    normal = jnp.where(
        core_index == 0,
        jnp.concatenate([mine, got], axis=1),
        jnp.concatenate([got, mine], axis=1),
    )
    return (normal, right_hand)


def solution(mesh):
    chips = mesh.devices.shape[0] // 2
    split = Mesh(
        mesh.devices.reshape(chips, 2, mesh.devices.shape[1]), ("tmc", "core", "panel")
    )
    in_specs = (P(TM, "panel"), P(TM, None), P(TM), P(), P(), P())
    out_specs = (P(TM, "panel"), P("panel"))
    return jax.shard_map(body, mesh=split, in_specs=in_specs, out_specs=out_specs, check_vma=False)
```

```python
import jax
import jax.numpy as jnp
from jax import lax
from jax.sharding import Mesh, PartitionSpec as P

TM = ("tmc", "core")


def whiten_matrix(order_row, order_col, usable_row, usable_col, ar_value, ma_value):
    spacing = order_row[:, None] - order_col[None, :]
    lag_steps = jnp.maximum(spacing - 1, 0)
    parity = (lag_steps % 2).astype(jnp.float32)
    flip_sign = 1.0 - 2.0 * parity
    decayed = (
        -(ar_value + ma_value)
        * flip_sign
        * jnp.exp(lag_steps.astype(jnp.float32) * jnp.log(ma_value))
    )
    entry = jnp.where(spacing == 0, jnp.float32(1.0), decayed)
    allowed = usable_row[:, None] & usable_col[None, :] & (spacing >= 0)
    return jnp.where(allowed, entry, jnp.float32(0.0)).astype(jnp.bfloat16)


def eliminate(whitener, rows_design, rows_params, rows_obs, scale):
    white_design = jnp.dot(whitener, rows_design, preferred_element_type=jnp.float32)
    white_params = jnp.dot(whitener, rows_params, preferred_element_type=jnp.float32)
    white_obs = jnp.dot(whitener, rows_obs, preferred_element_type=jnp.float32)
    param_count = rows_params.shape[1]
    param_gram = jnp.dot(white_params.T, white_params, precision=lax.Precision.HIGHEST) + jnp.eye(
        param_count, dtype=jnp.float32
    )
    factor = jnp.linalg.cholesky(param_gram)
    basis = lax.linalg.triangular_solve(factor, white_params.T, left_side=True, lower=True)
    arc_terms = jnp.dot(basis, white_design, precision=lax.Precision.HIGHEST)
    arc_rhs = jnp.dot(basis, white_obs, precision=lax.Precision.HIGHEST)
    right_part = (
        jnp.dot(white_design.T, white_obs, precision=lax.Precision.HIGHEST)
        - jnp.dot(arc_terms.T, arc_rhs, precision=lax.Precision.HIGHEST)
    ) * scale
    return (white_design.astype(jnp.bfloat16), basis, right_part)


def body(design, partials, observed, arc_of_row, autoreg, movavg):
    chip_count = lax.axis_size("tmc")
    core_count = lax.axis_size("core")
    core_index = lax.axis_index("core")
    tile_count = chip_count * core_count
    device_index = lax.axis_index("tmc") * core_count + core_index
    rows_dev = design.shape[0]
    panel_width = design.shape[1]
    param_count = partials.shape[1]
    capacity = 3 * rows_dev // 2 // tile_count
    slot_count = tile_count * capacity
    scale = 1.0 / (rows_dev * tile_count)
    arc_ids = arc_of_row[:, 0]
    epoch_table = arc_ids.reshape(rows_dev, tile_count)
    local_arcs = lax.dynamic_slice_in_dim(epoch_table, device_index, 1, 1)[:, 0]
    onehot = (local_arcs[:, None] == jnp.arange(tile_count, dtype=jnp.int32)[None, :]).astype(
        jnp.int32
    )
    earlier = jnp.cumsum(onehot, axis=0) - onehot
    within = jnp.sum(earlier * onehot, axis=1)
    target_slot = local_arcs * capacity + within
    chooser = (
        target_slot[None, :] == jnp.arange(slot_count, dtype=jnp.int32)[:, None]
    ).astype(jnp.bfloat16)

    def pick_rows(values):
        picked = jnp.dot(chooser, values, preferred_element_type=jnp.float32)
        return picked.astype(values.dtype)

    send_design = pick_rows(design).reshape(tile_count, capacity, panel_width)
    with_obs = jnp.concatenate([partials, observed[:, None]], axis=1)
    send_params = pick_rows(with_obs).reshape(tile_count, capacity, param_count + 1)
    got_params = lax.all_to_all(send_params, TM, split_axis=0, concat_axis=0, tiled=True)
    send_design, got_params = lax.optimization_barrier((send_design, got_params))
    got_design = lax.all_to_all(send_design, TM, split_axis=0, concat_axis=0, tiled=True)
    got_design = got_design.reshape(slot_count, panel_width)
    got_params = got_params.reshape(slot_count, param_count + 1)
    got_obs = got_params[:, param_count]
    got_params = got_params[:, :param_count]
    per_source = jnp.sum((epoch_table == device_index).astype(jnp.int32), axis=0)
    arc_start = jnp.sum((arc_ids < device_index).astype(jnp.int32))
    first_pos = jnp.mod(jnp.arange(tile_count, dtype=jnp.int32) - arc_start, tile_count)
    offset_in = jnp.arange(capacity, dtype=jnp.int32)
    order_pos = (first_pos[:, None] + offset_in[None, :] * tile_count).reshape(slot_count)
    usable = (offset_in[None, :] < per_source[:, None]).reshape(slot_count)
    position = jnp.arange(slot_count, dtype=jnp.int32)
    arc_length = jnp.sum(per_source)
    whitener = whiten_matrix(
        position, order_pos, position < arc_length, usable,
        autoreg[device_index], movavg[device_index],
    )
    design_bf, basis, right_part = eliminate(whitener, got_design, got_params, got_obs, scale)
    swap = [(0, 1), (1, 0)]
    short_most = 5 * rows_dev // 8
    keep = (slot_count + short_most) // 2
    moved = lax.ppermute(design_bf[keep:], "core", swap)
    packed = design_bf[:keep].at[short_most : short_most + moved.shape[0]].add(moved)
    got_basis = lax.ppermute(basis, "core", swap)
    packed, right_part, got_basis = lax.optimization_barrier((packed, right_part, got_basis))
    gathered = lax.all_gather(packed, "panel", axis=1, tiled=True)
    right_hand = lax.psum(right_part + lax.ppermute(right_part, "core", swap), "tmc")
    gathered, right_hand = lax.optimization_barrier((gathered, right_hand))
    half = panel_width // core_count
    got_rows = lax.ppermute(gathered, "core", swap)
    moved_count = slot_count - keep

    def spread(own_basis):
        lead = own_basis[:, :keep]
        tail = jnp.pad(own_basis[:, keep:], ((0, 0), (short_most, keep - short_most - moved_count)))
        return lead, tail

    own_lead, own_tail = spread(basis)
    far_lead, far_tail = spread(got_basis)
    stacked_basis = jnp.concatenate(
        [
            jnp.concatenate([own_lead, own_tail], axis=1),
            jnp.concatenate([far_tail, far_lead], axis=1),
        ],
        axis=0,
    ).astype(jnp.bfloat16)
    design_side = jnp.concatenate([gathered, got_rows], axis=0)
    terms = jnp.dot(stacked_basis, design_side, preferred_element_type=jnp.float32).astype(
        jnp.bfloat16
    )
    row_side = jnp.concatenate([design_side, -terms], axis=0)
    col_side = lax.dynamic_slice_in_dim(
        jnp.concatenate([design_side, terms], axis=0),
        lax.axis_index("panel") * panel_width + core_index * half, half, 1,
    )
    product = lax.dot_general(
        row_side, col_side, (((0,), (0,)), ((), ())), preferred_element_type=jnp.float32
    )
    pair = lax.psum_scatter(
        (product * scale).astype(jnp.bfloat16), "tmc", scatter_dimension=0, tiled=True
    )
    block_rows = pair.shape[0] // core_count
    by_core = pair.reshape(core_count, block_rows, half)
    mine = lax.dynamic_index_in_dim(by_core, core_index, 0, keepdims=False)
    given = lax.dynamic_index_in_dim(by_core, 1 - core_index, 0, keepdims=False)
    got = lax.ppermute(given, "core", swap)
    first = jnp.where(core_index == 0, mine, got)
    second = jnp.where(core_index == 0, got, mine)
    normal = jnp.concatenate([first, second], axis=1).astype(jnp.float32)
    return (normal, right_hand)


def solution(mesh):
    chips = mesh.devices.shape[0] // 2
    split = Mesh(
        mesh.devices.reshape(chips, 2, mesh.devices.shape[1]), ("tmc", "core", "panel")
    )
    in_specs = (P(TM, "panel"), P(TM, None), P(TM), P(), P(), P())
    out_specs = (P(TM, "panel"), P("panel"))
    return jax.shard_map(body, mesh=split, in_specs=in_specs, out_specs=out_specs, check_vma=False)
```

```python
import jax
import jax.numpy as jnp
from jax import lax
from jax.sharding import Mesh, PartitionSpec as P

TM = ("tmc", "core")


def whiten_matrix(order_row, order_col, usable_row, usable_col, ar_value, ma_value):
    spacing = order_row[:, None] - order_col[None, :]
    lag_steps = jnp.maximum(spacing - 1, 0)
    parity = (lag_steps % 2).astype(jnp.float32)
    flip_sign = 1.0 - 2.0 * parity
    decayed = (
        -(ar_value + ma_value)
        * flip_sign
        * jnp.exp(lag_steps.astype(jnp.float32) * jnp.log(ma_value))
    )
    entry = jnp.where(spacing == 0, jnp.float32(1.0), decayed)
    allowed = usable_row[:, None] & usable_col[None, :] & (spacing >= 0)
    return jnp.where(allowed, entry, jnp.float32(0.0)).astype(jnp.bfloat16)


def eliminate(whitener, rows_design, rows_params, rows_obs, scale):
    white_design = jnp.dot(whitener, rows_design, preferred_element_type=jnp.float32)
    white_params = jnp.dot(whitener, rows_params, preferred_element_type=jnp.float32)
    white_obs = jnp.dot(whitener, rows_obs, preferred_element_type=jnp.float32)
    param_count = rows_params.shape[1]
    param_gram = jnp.dot(white_params.T, white_params, precision=lax.Precision.HIGHEST) + jnp.eye(
        param_count, dtype=jnp.float32
    )
    factor = jnp.linalg.cholesky(param_gram)
    basis = lax.linalg.triangular_solve(factor, white_params.T, left_side=True, lower=True)
    arc_terms = jnp.dot(basis, white_design, precision=lax.Precision.HIGHEST)
    arc_rhs = jnp.dot(basis, white_obs, precision=lax.Precision.HIGHEST)
    right_part = (
        jnp.dot(white_design.T, white_obs, precision=lax.Precision.HIGHEST)
        - jnp.dot(arc_terms.T, arc_rhs, precision=lax.Precision.HIGHEST)
    ) * scale
    return (white_design.astype(jnp.bfloat16), basis, right_part)


def body(design, partials, observed, arc_of_row, autoreg, movavg):
    chip_count = lax.axis_size("tmc")
    core_count = lax.axis_size("core")
    core_index = lax.axis_index("core")
    tile_count = chip_count * core_count
    device_index = lax.axis_index("tmc") * core_count + core_index
    rows_dev = design.shape[0]
    panel_width = design.shape[1]
    param_count = partials.shape[1]
    capacity = 3 * rows_dev // 2 // tile_count
    slot_count = tile_count * capacity
    scale = 1.0 / (rows_dev * tile_count)
    arc_ids = arc_of_row[:, 0]
    epoch_table = arc_ids.reshape(rows_dev, tile_count)
    local_arcs = lax.dynamic_slice_in_dim(epoch_table, device_index, 1, 1)[:, 0]
    onehot = (local_arcs[:, None] == jnp.arange(tile_count, dtype=jnp.int32)[None, :]).astype(
        jnp.int32
    )
    earlier = jnp.cumsum(onehot, axis=0) - onehot
    within = jnp.sum(earlier * onehot, axis=1)
    target_slot = local_arcs * capacity + within
    chooser = (
        target_slot[None, :] == jnp.arange(slot_count, dtype=jnp.int32)[:, None]
    ).astype(jnp.bfloat16)

    def pick_rows(values):
        picked = jnp.dot(chooser, values, preferred_element_type=jnp.float32)
        return picked.astype(values.dtype)

    send_design = pick_rows(design).reshape(tile_count, capacity, panel_width)
    with_obs = jnp.concatenate([partials, observed[:, None]], axis=1)
    send_params = pick_rows(with_obs).reshape(tile_count, capacity, param_count + 1)
    got_params = lax.all_to_all(send_params, TM, split_axis=0, concat_axis=0, tiled=True)
    send_design, got_params = lax.optimization_barrier((send_design, got_params))
    got_design = lax.all_to_all(send_design, TM, split_axis=0, concat_axis=0, tiled=True)
    got_design = got_design.reshape(slot_count, panel_width)
    got_params = got_params.reshape(slot_count, param_count + 1)
    got_obs = got_params[:, param_count]
    got_params = got_params[:, :param_count]
    per_source = jnp.sum((epoch_table == device_index).astype(jnp.int32), axis=0)
    arc_start = jnp.sum((arc_ids < device_index).astype(jnp.int32))
    first_pos = jnp.mod(jnp.arange(tile_count, dtype=jnp.int32) - arc_start, tile_count)
    offset_in = jnp.arange(capacity, dtype=jnp.int32)
    order_pos = (first_pos[:, None] + offset_in[None, :] * tile_count).reshape(slot_count)
    usable = (offset_in[None, :] < per_source[:, None]).reshape(slot_count)
    position = jnp.arange(slot_count, dtype=jnp.int32)
    arc_length = jnp.sum(per_source)
    whitener = whiten_matrix(
        position, order_pos, position < arc_length, usable,
        autoreg[device_index], movavg[device_index],
    )
    design_bf, basis, right_part = eliminate(whitener, got_design, got_params, got_obs, scale)
    swap = [(0, 1), (1, 0)]
    short_most = 5 * rows_dev // 8
    keep = (slot_count + short_most) // 2
    moved = lax.ppermute(design_bf[keep:], "core", swap)
    packed = design_bf[:keep].at[short_most : short_most + moved.shape[0]].add(moved)
    got_basis = lax.ppermute(basis, "core", swap)
    packed, right_part, got_basis = lax.optimization_barrier((packed, right_part, got_basis))
    gathered = lax.all_gather(packed, "panel", axis=1, tiled=True)
    right_hand = lax.psum(right_part + lax.ppermute(right_part, "core", swap), "tmc")
    gathered, right_hand = lax.optimization_barrier((gathered, right_hand))
    half = panel_width // core_count
    got_rows = lax.ppermute(gathered, "core", swap)
    moved_count = slot_count - keep

    def spread(own_basis):
        lead = own_basis[:, :keep]
        tail = jnp.pad(own_basis[:, keep:], ((0, 0), (short_most, keep - short_most - moved_count)))
        return lead, tail

    own_lead, own_tail = spread(basis)
    far_lead, far_tail = spread(got_basis)
    stacked_basis = jnp.concatenate(
        [
            jnp.concatenate([own_lead, own_tail], axis=1),
            jnp.concatenate([far_tail, far_lead], axis=1),
        ],
        axis=0,
    ).astype(jnp.bfloat16)
    design_side = jnp.concatenate([gathered, got_rows], axis=0)
    own_share = jnp.dot(stacked_basis[:, :keep], gathered, preferred_element_type=jnp.float32)
    far_share = jnp.dot(stacked_basis[:, keep:], got_rows, preferred_element_type=jnp.float32)
    terms = (own_share + far_share).astype(jnp.bfloat16)
    row_side = jnp.concatenate([design_side, -terms], axis=0)
    col_side = lax.dynamic_slice_in_dim(
        jnp.concatenate([design_side, terms], axis=0),
        lax.axis_index("panel") * panel_width + core_index * half, half, 1,
    )
    product = lax.dot_general(
        row_side, col_side, (((0,), (0,)), ((), ())), preferred_element_type=jnp.float32
    )
    pair = lax.psum_scatter(
        (product * scale).astype(jnp.bfloat16), "tmc", scatter_dimension=0, tiled=True
    )
    block_rows = pair.shape[0] // core_count
    by_core = pair.reshape(core_count, block_rows, half)
    mine = lax.dynamic_index_in_dim(by_core, core_index, 0, keepdims=False)
    given = lax.dynamic_index_in_dim(by_core, 1 - core_index, 0, keepdims=False)
    got = lax.ppermute(given, "core", swap)
    first = jnp.where(core_index == 0, mine, got)
    second = jnp.where(core_index == 0, got, mine)
    normal = jnp.concatenate([first, second], axis=1).astype(jnp.float32)
    return (normal, right_hand)


def solution(mesh):
    chips = mesh.devices.shape[0] // 2
    split = Mesh(
        mesh.devices.reshape(chips, 2, mesh.devices.shape[1]), ("tmc", "core", "panel")
    )
    in_specs = (P(TM, "panel"), P(TM, None), P(TM), P(), P(), P())
    out_specs = (P(TM, "panel"), P("panel"))
    return jax.shard_map(body, mesh=split, in_specs=in_specs, out_specs=out_specs, check_vma=False)
```

```python
import jax
import jax.numpy as jnp
from jax import lax
from jax.sharding import Mesh, PartitionSpec as P

TM = ("tmc", "core")


def whiten_matrix(order_row, order_col, usable_row, usable_col, ar_value, ma_value):
    spacing = order_row[:, None] - order_col[None, :]
    lag_steps = jnp.maximum(spacing - 1, 0)
    parity = (lag_steps % 2).astype(jnp.float32)
    flip_sign = 1.0 - 2.0 * parity
    decayed = (
        -(ar_value + ma_value)
        * flip_sign
        * jnp.exp(lag_steps.astype(jnp.float32) * jnp.log(ma_value))
    )
    entry = jnp.where(spacing == 0, jnp.float32(1.0), decayed)
    allowed = usable_row[:, None] & usable_col[None, :] & (spacing >= 0)
    return jnp.where(allowed, entry, jnp.float32(0.0)).astype(jnp.bfloat16)


def eliminate(whitener, rows_design, rows_params, rows_obs, scale):
    white_design = jnp.dot(whitener, rows_design, preferred_element_type=jnp.float32)
    white_params = jnp.dot(whitener, rows_params, preferred_element_type=jnp.float32)
    white_obs = jnp.dot(whitener, rows_obs, preferred_element_type=jnp.float32)
    param_count = rows_params.shape[1]
    param_gram = jnp.dot(white_params.T, white_params, precision=lax.Precision.HIGHEST) + jnp.eye(
        param_count, dtype=jnp.float32
    )
    factor = jnp.linalg.cholesky(param_gram)
    basis = lax.linalg.triangular_solve(factor, white_params.T, left_side=True, lower=True)
    arc_terms = jnp.dot(basis, white_design, precision=lax.Precision.HIGHEST)
    arc_rhs = jnp.dot(basis, white_obs, precision=lax.Precision.HIGHEST)
    right_part = (
        jnp.dot(white_design.T, white_obs, precision=lax.Precision.HIGHEST)
        - jnp.dot(arc_terms.T, arc_rhs, precision=lax.Precision.HIGHEST)
    ) * scale
    return (white_design.astype(jnp.bfloat16), basis, right_part)


def body(design, partials, observed, arc_of_row, autoreg, movavg):
    chip_count = lax.axis_size("tmc")
    core_count = lax.axis_size("core")
    core_index = lax.axis_index("core")
    tile_count = chip_count * core_count
    device_index = lax.axis_index("tmc") * core_count + core_index
    rows_dev = design.shape[0]
    panel_width = design.shape[1]
    param_count = partials.shape[1]
    capacity = 3 * rows_dev // 2 // tile_count
    slot_count = tile_count * capacity
    scale = 1.0 / (rows_dev * tile_count)
    arc_ids = arc_of_row[:, 0]
    epoch_table = arc_ids.reshape(rows_dev, tile_count)
    local_arcs = lax.dynamic_slice_in_dim(epoch_table, device_index, 1, 1)[:, 0]
    onehot = (local_arcs[:, None] == jnp.arange(tile_count, dtype=jnp.int32)[None, :]).astype(
        jnp.int32
    )
    earlier = jnp.cumsum(onehot, axis=0) - onehot
    within = jnp.sum(earlier * onehot, axis=1)
    target_slot = local_arcs * capacity + within
    chooser = (
        target_slot[None, :] == jnp.arange(slot_count, dtype=jnp.int32)[:, None]
    ).astype(jnp.bfloat16)

    def pick_rows(values):
        picked = jnp.dot(chooser, values, preferred_element_type=jnp.float32)
        return picked.astype(values.dtype)

    send_design = pick_rows(design).reshape(tile_count, capacity, panel_width)
    with_obs = jnp.concatenate([partials, observed[:, None]], axis=1)
    send_params = pick_rows(with_obs).reshape(tile_count, capacity, param_count + 1)
    got_params = lax.all_to_all(send_params, TM, split_axis=0, concat_axis=0, tiled=True)
    send_design, got_params = lax.optimization_barrier((send_design, got_params))
    got_design = lax.all_to_all(send_design, TM, split_axis=0, concat_axis=0, tiled=True)
    got_design = got_design.reshape(slot_count, panel_width)
    got_params = got_params.reshape(slot_count, param_count + 1)
    got_obs = got_params[:, param_count]
    got_params = got_params[:, :param_count]
    per_source = jnp.sum((epoch_table == device_index).astype(jnp.int32), axis=0)
    arc_start = jnp.sum((arc_ids < device_index).astype(jnp.int32))
    first_pos = jnp.mod(jnp.arange(tile_count, dtype=jnp.int32) - arc_start, tile_count)
    offset_in = jnp.arange(capacity, dtype=jnp.int32)
    order_pos = (first_pos[:, None] + offset_in[None, :] * tile_count).reshape(slot_count)
    usable = (offset_in[None, :] < per_source[:, None]).reshape(slot_count)
    position = jnp.arange(slot_count, dtype=jnp.int32)
    arc_length = jnp.sum(per_source)
    whitener = whiten_matrix(
        position, order_pos, position < arc_length, usable,
        autoreg[device_index], movavg[device_index],
    )
    design_bf, basis, right_part = eliminate(whitener, got_design, got_params, got_obs, scale)
    swap = [(0, 1), (1, 0)]
    short_most = 5 * rows_dev // 8
    keep = (slot_count + short_most) // 2
    moved = lax.ppermute(design_bf[keep:], "core", swap)
    packed = design_bf[:keep].at[short_most : short_most + moved.shape[0]].add(moved)
    got_basis = lax.ppermute(basis, "core", swap)
    packed, got_basis = lax.optimization_barrier((packed, got_basis))
    gathered = lax.all_gather(packed, "panel", axis=1, tiled=True)
    right_hand = lax.psum(right_part + lax.ppermute(right_part, "core", swap), "tmc")
    gathered, right_hand = lax.optimization_barrier((gathered, right_hand))
    half = panel_width // core_count
    got_rows = lax.ppermute(gathered, "core", swap)
    moved_count = slot_count - keep

    def spread(own_basis):
        lead = own_basis[:, :keep]
        tail = jnp.pad(own_basis[:, keep:], ((0, 0), (short_most, keep - short_most - moved_count)))
        return lead, tail

    own_lead, own_tail = spread(basis)
    far_lead, far_tail = spread(got_basis)
    stacked_basis = jnp.concatenate(
        [
            jnp.concatenate([own_lead, own_tail], axis=1),
            jnp.concatenate([far_tail, far_lead], axis=1),
        ],
        axis=0,
    ).astype(jnp.bfloat16)
    design_side = jnp.concatenate([gathered, got_rows], axis=0)
    own_share = jnp.dot(stacked_basis[:, :keep], gathered, preferred_element_type=jnp.float32)
    far_share = jnp.dot(stacked_basis[:, keep:], got_rows, preferred_element_type=jnp.float32)
    terms = (own_share + far_share).astype(jnp.bfloat16)
    row_side = jnp.concatenate([design_side, -terms], axis=0)
    col_side = lax.dynamic_slice_in_dim(
        jnp.concatenate([design_side, terms], axis=0),
        lax.axis_index("panel") * panel_width + core_index * half, half, 1,
    )
    product = lax.dot_general(
        row_side, col_side, (((0,), (0,)), ((), ())), preferred_element_type=jnp.float32
    )
    pair = lax.psum_scatter(
        (product * scale).astype(jnp.bfloat16), "tmc", scatter_dimension=0, tiled=True
    )
    block_rows = pair.shape[0] // core_count
    by_core = pair.reshape(core_count, block_rows, half)
    mine = lax.dynamic_index_in_dim(by_core, core_index, 0, keepdims=False)
    given = lax.dynamic_index_in_dim(by_core, 1 - core_index, 0, keepdims=False)
    got = lax.ppermute(given, "core", swap)
    first = jnp.where(core_index == 0, mine, got)
    second = jnp.where(core_index == 0, got, mine)
    normal = jnp.concatenate([first, second], axis=1).astype(jnp.float32)
    return (normal, right_hand)


def solution(mesh):
    chips = mesh.devices.shape[0] // 2
    split = Mesh(
        mesh.devices.reshape(chips, 2, mesh.devices.shape[1]), ("tmc", "core", "panel")
    )
    in_specs = (P(TM, "panel"), P(TM, None), P(TM), P(), P(), P())
    out_specs = (P(TM, "panel"), P("panel"))
    return jax.shard_map(body, mesh=split, in_specs=in_specs, out_specs=out_specs, check_vma=False)
```

```python
import jax
import jax.numpy as jnp
from jax import lax
from jax.sharding import Mesh, PartitionSpec as P

TM = ("tmc", "core")


def whiten_matrix(order_row, order_col, usable_row, usable_col, ar_value, ma_value):
    spacing = order_row[:, None] - order_col[None, :]
    lag_steps = jnp.maximum(spacing - 1, 0)
    parity = (lag_steps % 2).astype(jnp.float32)
    flip_sign = 1.0 - 2.0 * parity
    decayed = (
        -(ar_value + ma_value)
        * flip_sign
        * jnp.exp(lag_steps.astype(jnp.float32) * jnp.log(ma_value))
    )
    entry = jnp.where(spacing == 0, jnp.float32(1.0), decayed)
    allowed = usable_row[:, None] & usable_col[None, :] & (spacing >= 0)
    return jnp.where(allowed, entry, jnp.float32(0.0)).astype(jnp.bfloat16)


def eliminate(whitener, rows_design, rows_params, rows_obs, scale):
    white_design = jnp.dot(whitener, rows_design, preferred_element_type=jnp.float32)
    white_params = jnp.dot(whitener, rows_params, preferred_element_type=jnp.float32)
    white_obs = jnp.dot(whitener, rows_obs, preferred_element_type=jnp.float32)
    param_count = rows_params.shape[1]
    param_gram = jnp.dot(white_params.T, white_params, precision=lax.Precision.HIGHEST) + jnp.eye(
        param_count, dtype=jnp.float32
    )
    factor = jnp.linalg.cholesky(param_gram)
    basis = lax.linalg.triangular_solve(factor, white_params.T, left_side=True, lower=True)
    arc_terms = jnp.dot(basis, white_design, precision=lax.Precision.HIGHEST)
    arc_rhs = jnp.dot(basis, white_obs, precision=lax.Precision.HIGHEST)
    right_part = (
        jnp.dot(white_design.T, white_obs, precision=lax.Precision.HIGHEST)
        - jnp.dot(arc_terms.T, arc_rhs, precision=lax.Precision.HIGHEST)
    ) * scale
    return (white_design.astype(jnp.bfloat16), basis, right_part)


def body(design, partials, observed, arc_of_row, autoreg, movavg):
    chip_count = lax.axis_size("tmc")
    core_count = lax.axis_size("core")
    core_index = lax.axis_index("core")
    tile_count = chip_count * core_count
    device_index = lax.axis_index("tmc") * core_count + core_index
    rows_dev = design.shape[0]
    panel_width = design.shape[1]
    param_count = partials.shape[1]
    capacity = 3 * rows_dev // 2 // tile_count
    slot_count = tile_count * capacity
    scale = 1.0 / (rows_dev * tile_count)
    arc_ids = arc_of_row[:, 0]
    epoch_table = arc_ids.reshape(rows_dev, tile_count)
    local_arcs = lax.dynamic_slice_in_dim(epoch_table, device_index, 1, 1)[:, 0]
    onehot = (local_arcs[:, None] == jnp.arange(tile_count, dtype=jnp.int32)[None, :]).astype(
        jnp.int32
    )
    earlier = jnp.cumsum(onehot, axis=0) - onehot
    within = jnp.sum(earlier * onehot, axis=1)
    target_slot = local_arcs * capacity + within
    chooser = (
        target_slot[None, :] == jnp.arange(slot_count, dtype=jnp.int32)[:, None]
    ).astype(jnp.bfloat16)

    def pick_rows(values):
        picked = jnp.dot(chooser, values, preferred_element_type=jnp.float32)
        return picked.astype(values.dtype)

    send_design = pick_rows(design).reshape(tile_count, capacity, panel_width)
    with_obs = jnp.concatenate([partials, observed[:, None]], axis=1)
    send_params = pick_rows(with_obs).reshape(tile_count, capacity, param_count + 1)
    got_params = lax.all_to_all(send_params, TM, split_axis=0, concat_axis=0, tiled=True)
    send_design, got_params = lax.optimization_barrier((send_design, got_params))
    got_design = lax.all_to_all(send_design, TM, split_axis=0, concat_axis=0, tiled=True)
    got_design = got_design.reshape(slot_count, panel_width)
    got_params = got_params.reshape(slot_count, param_count + 1)
    got_obs = got_params[:, param_count]
    got_params = got_params[:, :param_count]
    per_source = jnp.sum((epoch_table == device_index).astype(jnp.int32), axis=0)
    arc_start = jnp.sum((arc_ids < device_index).astype(jnp.int32))
    first_pos = jnp.mod(jnp.arange(tile_count, dtype=jnp.int32) - arc_start, tile_count)
    offset_in = jnp.arange(capacity, dtype=jnp.int32)
    order_pos = (first_pos[:, None] + offset_in[None, :] * tile_count).reshape(slot_count)
    usable = (offset_in[None, :] < per_source[:, None]).reshape(slot_count)
    position = jnp.arange(slot_count, dtype=jnp.int32)
    arc_length = jnp.sum(per_source)
    whitener = whiten_matrix(
        position, order_pos, position < arc_length, usable,
        autoreg[device_index], movavg[device_index],
    )
    design_bf, basis, right_part = eliminate(whitener, got_design, got_params, got_obs, scale)
    swap = [(0, 1), (1, 0)]
    short_most = 5 * rows_dev // 8
    keep = (slot_count + short_most) // 2
    moved = lax.ppermute(design_bf[keep:], "core", swap)
    packed = design_bf[:keep].at[short_most : short_most + moved.shape[0]].add(moved)
    got_basis = lax.ppermute(basis, "core", swap)
    packed, right_part, got_basis = lax.optimization_barrier((packed, right_part, got_basis))
    gathered = lax.all_gather(packed, "panel", axis=1, tiled=True)
    right_hand = lax.psum(right_part + lax.ppermute(right_part, "core", swap), "tmc")
    gathered, right_hand = lax.optimization_barrier((gathered, right_hand))
    half = panel_width // core_count
    got_rows = lax.ppermute(gathered, "core", swap)
    moved_count = slot_count - keep

    def spread(own_basis):
        lead = own_basis[:, :keep]
        tail = jnp.pad(own_basis[:, keep:], ((0, 0), (short_most, keep - short_most - moved_count)))
        return lead, tail

    own_lead, own_tail = spread(basis)
    far_lead, far_tail = spread(got_basis)
    stacked_basis = jnp.concatenate(
        [
            jnp.concatenate([own_lead, own_tail], axis=1),
            jnp.concatenate([far_tail, far_lead], axis=1),
        ],
        axis=0,
    ).astype(jnp.bfloat16)
    design_side = jnp.concatenate([gathered, got_rows], axis=0)
    own_share = jnp.dot(stacked_basis[:, :keep], gathered, preferred_element_type=jnp.float32)
    far_share = lax.ppermute(own_share, "core", swap)
    far_share = jnp.concatenate([far_share[own_lead.shape[0] :], far_share[: own_lead.shape[0]]], axis=0)
    terms = (own_share + far_share).astype(jnp.bfloat16)
    row_side = jnp.concatenate([design_side, -terms], axis=0)
    col_side = lax.dynamic_slice_in_dim(
        jnp.concatenate([design_side, terms], axis=0),
        lax.axis_index("panel") * panel_width + core_index * half, half, 1,
    )
    product = lax.dot_general(
        row_side, col_side, (((0,), (0,)), ((), ())), preferred_element_type=jnp.float32
    )
    pair = lax.psum_scatter(
        (product * scale).astype(jnp.bfloat16), "tmc", scatter_dimension=0, tiled=True
    )
    block_rows = pair.shape[0] // core_count
    by_core = pair.reshape(core_count, block_rows, half)
    mine = lax.dynamic_index_in_dim(by_core, core_index, 0, keepdims=False)
    given = lax.dynamic_index_in_dim(by_core, 1 - core_index, 0, keepdims=False)
    got = lax.ppermute(given, "core", swap)
    first = jnp.where(core_index == 0, mine, got)
    second = jnp.where(core_index == 0, got, mine)
    normal = jnp.concatenate([first, second], axis=1).astype(jnp.float32)
    return (normal, right_hand)


def solution(mesh):
    chips = mesh.devices.shape[0] // 2
    split = Mesh(
        mesh.devices.reshape(chips, 2, mesh.devices.shape[1]), ("tmc", "core", "panel")
    )
    in_specs = (P(TM, "panel"), P(TM, None), P(TM), P(), P(), P())
    out_specs = (P(TM, "panel"), P("panel"))
    return jax.shard_map(body, mesh=split, in_specs=in_specs, out_specs=out_specs, check_vma=False)
```

```python
import jax
import jax.numpy as jnp
from jax import lax
from jax.sharding import Mesh, PartitionSpec as P

TM = ("tmc", "core")


def whiten_matrix(order_row, order_col, usable_row, usable_col, ar_value, ma_value):
    spacing = order_row[:, None] - order_col[None, :]
    lag_steps = jnp.maximum(spacing - 1, 0)
    parity = (lag_steps % 2).astype(jnp.float32)
    flip_sign = 1.0 - 2.0 * parity
    decayed = (
        -(ar_value + ma_value)
        * flip_sign
        * jnp.exp(lag_steps.astype(jnp.float32) * jnp.log(ma_value))
    )
    entry = jnp.where(spacing == 0, jnp.float32(1.0), decayed)
    allowed = usable_row[:, None] & usable_col[None, :] & (spacing >= 0)
    return jnp.where(allowed, entry, jnp.float32(0.0)).astype(jnp.bfloat16)


def eliminate(whitener, rows_design, rows_params, rows_obs, scale):
    white_design = jnp.dot(whitener, rows_design, preferred_element_type=jnp.float32)
    white_params = jnp.dot(whitener, rows_params, preferred_element_type=jnp.float32)
    white_obs = jnp.dot(whitener, rows_obs, preferred_element_type=jnp.float32)
    param_count = rows_params.shape[1]
    param_gram = jnp.dot(white_params.T, white_params, precision=lax.Precision.HIGHEST) + jnp.eye(
        param_count, dtype=jnp.float32
    )
    factor = jnp.linalg.cholesky(param_gram)
    basis = lax.linalg.triangular_solve(factor, white_params.T, left_side=True, lower=True)
    arc_terms = jnp.dot(basis, white_design, precision=lax.Precision.HIGHEST)
    arc_rhs = jnp.dot(basis, white_obs, precision=lax.Precision.HIGHEST)
    right_part = (
        jnp.dot(white_design.T, white_obs, precision=lax.Precision.HIGHEST)
        - jnp.dot(arc_terms.T, arc_rhs, precision=lax.Precision.HIGHEST)
    ) * scale
    return (white_design.astype(jnp.bfloat16), basis, right_part)


def body(design, partials, observed, arc_of_row, autoreg, movavg):
    chip_count = lax.axis_size("tmc")
    core_count = lax.axis_size("core")
    core_index = lax.axis_index("core")
    tile_count = chip_count * core_count
    device_index = lax.axis_index("tmc") * core_count + core_index
    rows_dev = design.shape[0]
    panel_width = design.shape[1]
    param_count = partials.shape[1]
    capacity = 3 * rows_dev // 2 // tile_count
    slot_count = tile_count * capacity
    scale = 1.0 / (rows_dev * tile_count)
    arc_ids = arc_of_row[:, 0]
    epoch_table = arc_ids.reshape(rows_dev, tile_count)
    local_arcs = lax.dynamic_slice_in_dim(epoch_table, device_index, 1, 1)[:, 0]
    row_id = jnp.arange(rows_dev, dtype=jnp.int32)
    same_arc = local_arcs[:, None] == local_arcs[None, :]
    within = jnp.sum((same_arc & (row_id[None, :] < row_id[:, None])).astype(jnp.int32), axis=1)
    target_slot = local_arcs * capacity + within
    chooser = (
        target_slot[None, :] == jnp.arange(slot_count, dtype=jnp.int32)[:, None]
    ).astype(jnp.bfloat16)

    def pick_rows(values):
        picked = jnp.dot(chooser, values, preferred_element_type=jnp.float32)
        return picked.astype(values.dtype)

    send_design = pick_rows(design).reshape(tile_count, capacity, panel_width)
    with_obs = jnp.concatenate([partials, observed[:, None]], axis=1)
    send_params = pick_rows(with_obs).reshape(tile_count, capacity, param_count + 1)
    got_params = lax.all_to_all(send_params, TM, split_axis=0, concat_axis=0, tiled=True)
    send_design, got_params = lax.optimization_barrier((send_design, got_params))
    got_design = lax.all_to_all(send_design, TM, split_axis=0, concat_axis=0, tiled=True)
    got_design = got_design.reshape(slot_count, panel_width)
    got_params = got_params.reshape(slot_count, param_count + 1)
    got_obs = got_params[:, param_count]
    got_params = got_params[:, :param_count]
    per_source = jnp.sum((epoch_table == device_index).astype(jnp.int32), axis=0)
    arc_start = jnp.sum((arc_ids < device_index).astype(jnp.int32))
    first_pos = jnp.mod(jnp.arange(tile_count, dtype=jnp.int32) - arc_start, tile_count)
    offset_in = jnp.arange(capacity, dtype=jnp.int32)
    order_pos = (first_pos[:, None] + offset_in[None, :] * tile_count).reshape(slot_count)
    usable = (offset_in[None, :] < per_source[:, None]).reshape(slot_count)
    position = jnp.arange(slot_count, dtype=jnp.int32)
    arc_length = jnp.sum(per_source)
    whitener = whiten_matrix(
        position, order_pos, position < arc_length, usable,
        autoreg[device_index], movavg[device_index],
    )
    design_bf, basis, right_part = eliminate(whitener, got_design, got_params, got_obs, scale)
    swap = [(0, 1), (1, 0)]
    short_most = 5 * rows_dev // 8
    keep = (slot_count + short_most) // 2
    moved = lax.ppermute(design_bf[keep:], "core", swap)
    packed = design_bf[:keep].at[short_most : short_most + moved.shape[0]].add(moved)
    got_basis = lax.ppermute(basis, "core", swap)
    packed, right_part, got_basis = lax.optimization_barrier((packed, right_part, got_basis))
    gathered = lax.all_gather(packed, "panel", axis=1, tiled=True)
    right_hand = lax.psum(right_part + lax.ppermute(right_part, "core", swap), "tmc")
    gathered, right_hand = lax.optimization_barrier((gathered, right_hand))
    half = panel_width // core_count
    got_rows = lax.ppermute(gathered, "core", swap)
    moved_count = slot_count - keep

    def spread(own_basis):
        lead = own_basis[:, :keep]
        tail = jnp.pad(own_basis[:, keep:], ((0, 0), (short_most, keep - short_most - moved_count)))
        return lead, tail

    own_lead, own_tail = spread(basis)
    far_lead, far_tail = spread(got_basis)
    stacked_basis = jnp.concatenate(
        [
            jnp.concatenate([own_lead, own_tail], axis=1),
            jnp.concatenate([far_tail, far_lead], axis=1),
        ],
        axis=0,
    ).astype(jnp.bfloat16)
    design_side = jnp.concatenate([gathered, got_rows], axis=0)
    own_share = jnp.dot(stacked_basis[:, :keep], gathered, preferred_element_type=jnp.float32)
    far_share = jnp.dot(stacked_basis[:, keep:], got_rows, preferred_element_type=jnp.float32)
    terms = (own_share + far_share).astype(jnp.bfloat16)
    row_side = jnp.concatenate([design_side, -terms], axis=0)
    col_side = lax.dynamic_slice_in_dim(
        jnp.concatenate([design_side, terms], axis=0),
        lax.axis_index("panel") * panel_width + core_index * half, half, 1,
    )
    product = lax.dot_general(
        row_side, col_side, (((0,), (0,)), ((), ())), preferred_element_type=jnp.float32
    )
    pair = lax.psum_scatter(
        (product * scale).astype(jnp.bfloat16), "tmc", scatter_dimension=0, tiled=True
    )
    block_rows = pair.shape[0] // core_count
    by_core = pair.reshape(core_count, block_rows, half)
    mine = lax.dynamic_index_in_dim(by_core, core_index, 0, keepdims=False)
    given = lax.dynamic_index_in_dim(by_core, 1 - core_index, 0, keepdims=False)
    got = lax.ppermute(given, "core", swap)
    first = jnp.where(core_index == 0, mine, got)
    second = jnp.where(core_index == 0, got, mine)
    normal = jnp.concatenate([first, second], axis=1).astype(jnp.float32)
    return (normal, right_hand)


def solution(mesh):
    chips = mesh.devices.shape[0] // 2
    split = Mesh(
        mesh.devices.reshape(chips, 2, mesh.devices.shape[1]), ("tmc", "core", "panel")
    )
    in_specs = (P(TM, "panel"), P(TM, None), P(TM), P(), P(), P())
    out_specs = (P(TM, "panel"), P("panel"))
    return jax.shard_map(body, mesh=split, in_specs=in_specs, out_specs=out_specs, check_vma=False)
```

```python
import jax
import jax.numpy as jnp
from jax import lax
from jax.sharding import Mesh, PartitionSpec as P

TM = ("tmc", "core")


def whiten_matrix(order_row, order_col, usable_row, usable_col, ar_value, ma_value):
    spacing = order_row[:, None] - order_col[None, :]
    lag_steps = jnp.maximum(spacing - 1, 0)
    parity = (lag_steps % 2).astype(jnp.float32)
    flip_sign = 1.0 - 2.0 * parity
    decayed = (
        -(ar_value + ma_value)
        * flip_sign
        * jnp.exp(lag_steps.astype(jnp.float32) * jnp.log(ma_value))
    )
    entry = jnp.where(spacing == 0, jnp.float32(1.0), decayed)
    allowed = usable_row[:, None] & usable_col[None, :] & (spacing >= 0)
    return jnp.where(allowed, entry, jnp.float32(0.0)).astype(jnp.bfloat16)


def eliminate(whitener, rows_design, rows_params, rows_obs, scale):
    white_design = jnp.dot(whitener, rows_design, preferred_element_type=jnp.float32)
    white_params = jnp.dot(whitener, rows_params, preferred_element_type=jnp.float32)
    white_obs = jnp.dot(whitener, rows_obs, preferred_element_type=jnp.float32)
    param_count = rows_params.shape[1]
    param_gram = jnp.dot(white_params.T, white_params, precision=lax.Precision.HIGHEST) + jnp.eye(
        param_count, dtype=jnp.float32
    )
    factor = jnp.linalg.cholesky(param_gram)
    basis = lax.linalg.triangular_solve(factor, white_params.T, left_side=True, lower=True)
    arc_terms = jnp.dot(basis, white_design, precision=lax.Precision.HIGHEST)
    arc_rhs = jnp.dot(basis, white_obs, precision=lax.Precision.HIGHEST)
    right_part = (
        jnp.dot(white_design.T, white_obs, precision=lax.Precision.HIGHEST)
        - jnp.dot(arc_terms.T, arc_rhs, precision=lax.Precision.HIGHEST)
    ) * scale
    return (white_design.astype(jnp.bfloat16), basis, right_part)


def body(design, partials, observed, arc_of_row, autoreg, movavg):
    chip_count = lax.axis_size("tmc")
    core_count = lax.axis_size("core")
    core_index = lax.axis_index("core")
    tile_count = chip_count * core_count
    device_index = lax.axis_index("tmc") * core_count + core_index
    rows_dev = design.shape[0]
    panel_width = design.shape[1]
    param_count = partials.shape[1]
    capacity = 3 * rows_dev // 2 // tile_count
    slot_count = tile_count * capacity
    scale = 1.0 / (rows_dev * tile_count)
    arc_ids = arc_of_row[:, 0]
    epoch_table = arc_ids.reshape(rows_dev, tile_count)
    local_arcs = lax.dynamic_slice_in_dim(epoch_table, device_index, 1, 1)[:, 0]
    row_id = jnp.arange(rows_dev, dtype=jnp.int32)
    same_arc = local_arcs[:, None] == local_arcs[None, :]
    within = jnp.sum((same_arc & (row_id[None, :] < row_id[:, None])).astype(jnp.int32), axis=1)
    target_slot = local_arcs * capacity + within
    chooser = (
        target_slot[None, :] == jnp.arange(slot_count, dtype=jnp.int32)[:, None]
    ).astype(jnp.bfloat16)

    def pick_rows(values):
        picked = jnp.dot(chooser, values, preferred_element_type=jnp.float32)
        return picked.astype(values.dtype)

    send_design = pick_rows(design).reshape(tile_count, capacity, panel_width)
    with_obs = jnp.concatenate([partials, observed[:, None]], axis=1)
    send_params = pick_rows(with_obs).reshape(tile_count, capacity, param_count + 1)
    got_params = lax.all_to_all(send_params, TM, split_axis=0, concat_axis=0, tiled=True)
    send_design, got_params = lax.optimization_barrier((send_design, got_params))
    got_design = lax.all_to_all(send_design, TM, split_axis=0, concat_axis=0, tiled=True)
    got_design = got_design.reshape(slot_count, panel_width)
    got_params = got_params.reshape(slot_count, param_count + 1)
    got_obs = got_params[:, param_count]
    got_params = got_params[:, :param_count]
    per_source = jnp.sum((epoch_table == device_index).astype(jnp.int32), axis=0)
    arc_start = jnp.sum((arc_ids < device_index).astype(jnp.int32))
    first_pos = jnp.mod(jnp.arange(tile_count, dtype=jnp.int32) - arc_start, tile_count)
    offset_in = jnp.arange(capacity, dtype=jnp.int32)
    order_pos = (first_pos[:, None] + offset_in[None, :] * tile_count).reshape(slot_count)
    usable = (offset_in[None, :] < per_source[:, None]).reshape(slot_count)
    position = jnp.arange(slot_count, dtype=jnp.int32)
    arc_length = jnp.sum(per_source)
    whitener = whiten_matrix(
        position, order_pos, position < arc_length, usable,
        autoreg[device_index], movavg[device_index],
    )
    design_bf, basis, right_part = eliminate(whitener, got_design, got_params, got_obs, scale)
    swap = [(0, 1), (1, 0)]
    short_most = 5 * rows_dev // 8
    keep = (slot_count + short_most) // 2
    moved = lax.ppermute(design_bf[keep:], "core", swap)
    packed = design_bf[:keep].at[short_most : short_most + moved.shape[0]].add(moved)
    got_basis = lax.ppermute(basis, "core", swap)
    packed, right_part, got_basis = lax.optimization_barrier((packed, right_part, got_basis))
    gathered = lax.all_gather(packed, "panel", axis=1, tiled=True)
    right_hand = lax.psum(right_part + lax.ppermute(right_part, "core", swap), "tmc")
    gathered, right_hand = lax.optimization_barrier((gathered, right_hand))
    half = panel_width // core_count
    got_rows = lax.ppermute(gathered, "core", swap)
    moved_count = slot_count - keep

    def spread(own_basis):
        lead = own_basis[:, :keep]
        tail = jnp.pad(own_basis[:, keep:], ((0, 0), (short_most, keep - short_most - moved_count)))
        return lead, tail

    own_lead, own_tail = spread(basis)
    far_lead, far_tail = spread(got_basis)
    stacked_basis = jnp.concatenate(
        [
            jnp.concatenate([own_lead, own_tail], axis=1),
            jnp.concatenate([far_tail, far_lead], axis=1),
        ],
        axis=0,
    ).astype(jnp.bfloat16)
    design_side = jnp.concatenate([gathered, got_rows], axis=0)
    own_share = jnp.dot(stacked_basis[:, :keep], gathered, preferred_element_type=jnp.float32)
    far_share = jnp.dot(stacked_basis[:, keep:], got_rows, preferred_element_type=jnp.float32)
    terms = (own_share + far_share).astype(jnp.bfloat16)
    row_side = jnp.concatenate([design_side, -terms], axis=0)
    col_side = lax.dynamic_slice_in_dim(
        jnp.concatenate([design_side, terms], axis=0),
        lax.axis_index("panel") * panel_width + core_index * half, half, 1,
    )
    product = lax.dot_general(
        row_side, col_side, (((0,), (0,)), ((), ())), preferred_element_type=jnp.float32
    )
    pair = lax.psum_scatter(
        (product * scale).astype(jnp.bfloat16), "tmc", scatter_dimension=0, tiled=True
    )
    block_rows = pair.shape[0] // core_count
    by_core = pair.reshape(core_count, block_rows, half)
    mine = jnp.where(core_index == 0, by_core[0], by_core[1])
    given = jnp.where(core_index == 0, by_core[1], by_core[0])
    got = lax.ppermute(given, "core", swap)
    first = jnp.where(core_index == 0, mine, got)
    second = jnp.where(core_index == 0, got, mine)
    normal = jnp.concatenate([first, second], axis=1).astype(jnp.float32)
    return (normal, right_hand)


def solution(mesh):
    chips = mesh.devices.shape[0] // 2
    split = Mesh(
        mesh.devices.reshape(chips, 2, mesh.devices.shape[1]), ("tmc", "core", "panel")
    )
    in_specs = (P(TM, "panel"), P(TM, None), P(TM), P(), P(), P())
    out_specs = (P(TM, "panel"), P("panel"))
    return jax.shard_map(body, mesh=split, in_specs=in_specs, out_specs=out_specs, check_vma=False)
```

```python
import jax
import jax.numpy as jnp
from jax import lax
from jax.sharding import Mesh, PartitionSpec as P

TM = ("tmc", "core")


def whiten_matrix(order_row, order_col, usable_row, usable_col, ar_value, ma_value):
    spacing = order_row[:, None] - order_col[None, :]
    lag_steps = jnp.maximum(spacing - 1, 0)
    parity = (lag_steps % 2).astype(jnp.float32)
    flip_sign = 1.0 - 2.0 * parity
    decayed = (
        -(ar_value + ma_value)
        * flip_sign
        * jnp.exp(lag_steps.astype(jnp.float32) * jnp.log(ma_value))
    )
    entry = jnp.where(spacing == 0, jnp.float32(1.0), decayed)
    allowed = usable_row[:, None] & usable_col[None, :] & (spacing >= 0)
    return jnp.where(allowed, entry, jnp.float32(0.0)).astype(jnp.bfloat16)


def eliminate(whitener, rows_design, rows_params, rows_obs, scale):
    white_design = jnp.dot(whitener, rows_design, preferred_element_type=jnp.float32)
    white_params = jnp.dot(whitener, rows_params, preferred_element_type=jnp.float32)
    white_obs = jnp.dot(whitener, rows_obs, preferred_element_type=jnp.float32)
    param_count = rows_params.shape[1]
    param_gram = jnp.dot(white_params.T, white_params, precision=lax.Precision.HIGHEST) + jnp.eye(
        param_count, dtype=jnp.float32
    )
    factor = jnp.linalg.cholesky(param_gram)
    basis = lax.linalg.triangular_solve(factor, white_params.T, left_side=True, lower=True)
    arc_terms = jnp.dot(basis, white_design, precision=lax.Precision.HIGHEST)
    arc_rhs = jnp.dot(basis, white_obs, precision=lax.Precision.HIGHEST)
    right_part = (
        jnp.dot(white_design.T, white_obs, precision=lax.Precision.HIGHEST)
        - jnp.dot(arc_terms.T, arc_rhs, precision=lax.Precision.HIGHEST)
    ) * scale
    return (white_design.astype(jnp.bfloat16), basis, right_part)


def body(design, partials, observed, arc_of_row, autoreg, movavg):
    chip_count = lax.axis_size("tmc")
    core_count = lax.axis_size("core")
    core_index = lax.axis_index("core")
    tile_count = chip_count * core_count
    device_index = lax.axis_index("tmc") * core_count + core_index
    rows_dev = design.shape[0]
    panel_width = design.shape[1]
    param_count = partials.shape[1]
    capacity = 3 * rows_dev // 2 // tile_count
    slot_count = tile_count * capacity
    scale = 1.0 / (rows_dev * tile_count)
    arc_ids = arc_of_row[:, 0]
    epoch_table = arc_ids.reshape(rows_dev, tile_count)
    local_arcs = lax.dynamic_slice_in_dim(epoch_table, device_index, 1, 1)[:, 0]
    row_id = jnp.arange(rows_dev, dtype=jnp.int32)
    same_arc = local_arcs[:, None] == local_arcs[None, :]
    within = jnp.sum((same_arc & (row_id[None, :] < row_id[:, None])).astype(jnp.int32), axis=1)
    target_slot = local_arcs * capacity + within
    chooser = (
        target_slot[None, :] == jnp.arange(slot_count, dtype=jnp.int32)[:, None]
    ).astype(jnp.bfloat16)

    def pick_rows(values):
        picked = jnp.dot(chooser, values, preferred_element_type=jnp.float32)
        return picked.astype(values.dtype)

    send_design = pick_rows(design).reshape(tile_count, capacity, panel_width)
    lane_width = -(-(param_count + 1) // 128) * 128
    with_obs = jnp.concatenate(
        [partials, observed[:, None], jnp.zeros((rows_dev, lane_width - param_count - 1), partials.dtype)],
        axis=1,
    )
    send_params = pick_rows(with_obs).reshape(tile_count, capacity, lane_width)
    got_params = lax.all_to_all(send_params, TM, split_axis=0, concat_axis=0, tiled=True)
    send_design, got_params = lax.optimization_barrier((send_design, got_params))
    got_design = lax.all_to_all(send_design, TM, split_axis=0, concat_axis=0, tiled=True)
    got_design = got_design.reshape(slot_count, panel_width)
    got_params = got_params.reshape(slot_count, lane_width)
    got_obs = got_params[:, param_count]
    got_params = got_params[:, :param_count]
    per_source = jnp.sum((epoch_table == device_index).astype(jnp.int32), axis=0)
    arc_start = jnp.sum((arc_ids < device_index).astype(jnp.int32))
    first_pos = jnp.mod(jnp.arange(tile_count, dtype=jnp.int32) - arc_start, tile_count)
    offset_in = jnp.arange(capacity, dtype=jnp.int32)
    order_pos = (first_pos[:, None] + offset_in[None, :] * tile_count).reshape(slot_count)
    usable = (offset_in[None, :] < per_source[:, None]).reshape(slot_count)
    position = jnp.arange(slot_count, dtype=jnp.int32)
    arc_length = jnp.sum(per_source)
    whitener = whiten_matrix(
        position, order_pos, position < arc_length, usable,
        autoreg[device_index], movavg[device_index],
    )
    design_bf, basis, right_part = eliminate(whitener, got_design, got_params, got_obs, scale)
    swap = [(0, 1), (1, 0)]
    short_most = 5 * rows_dev // 8
    keep = (slot_count + short_most) // 2
    moved = lax.ppermute(design_bf[keep:], "core", swap)
    packed = design_bf[:keep].at[short_most : short_most + moved.shape[0]].add(moved)
    got_basis = lax.ppermute(basis, "core", swap)
    packed, right_part, got_basis = lax.optimization_barrier((packed, right_part, got_basis))
    gathered = lax.all_gather(packed, "panel", axis=1, tiled=True)
    right_hand = lax.psum(right_part + lax.ppermute(right_part, "core", swap), "tmc")
    gathered, right_hand = lax.optimization_barrier((gathered, right_hand))
    half = panel_width // core_count
    got_rows = lax.ppermute(gathered, "core", swap)
    moved_count = slot_count - keep

    def spread(own_basis):
        lead = own_basis[:, :keep]
        tail = jnp.pad(own_basis[:, keep:], ((0, 0), (short_most, keep - short_most - moved_count)))
        return lead, tail

    own_lead, own_tail = spread(basis)
    far_lead, far_tail = spread(got_basis)
    stacked_basis = jnp.concatenate(
        [
            jnp.concatenate([own_lead, own_tail], axis=1),
            jnp.concatenate([far_tail, far_lead], axis=1),
        ],
        axis=0,
    ).astype(jnp.bfloat16)
    design_side = jnp.concatenate([gathered, got_rows], axis=0)
    own_share = jnp.dot(stacked_basis[:, :keep], gathered, preferred_element_type=jnp.float32)
    far_share = jnp.dot(stacked_basis[:, keep:], got_rows, preferred_element_type=jnp.float32)
    terms = (own_share + far_share).astype(jnp.bfloat16)
    row_side = jnp.concatenate([design_side, -terms], axis=0)
    col_side = lax.dynamic_slice_in_dim(
        jnp.concatenate([design_side, terms], axis=0),
        lax.axis_index("panel") * panel_width + core_index * half, half, 1,
    )
    product = lax.dot_general(
        row_side, col_side, (((0,), (0,)), ((), ())), preferred_element_type=jnp.float32
    )
    pair = lax.psum_scatter(
        (product * scale).astype(jnp.bfloat16), "tmc", scatter_dimension=0, tiled=True
    )
    block_rows = pair.shape[0] // core_count
    by_core = pair.reshape(core_count, block_rows, half)
    mine = jnp.where(core_index == 0, by_core[0], by_core[1])
    given = jnp.where(core_index == 0, by_core[1], by_core[0])
    got = lax.ppermute(given, "core", swap)
    first = jnp.where(core_index == 0, mine, got)
    second = jnp.where(core_index == 0, got, mine)
    normal = jnp.concatenate([first, second], axis=1).astype(jnp.float32)
    return (normal, right_hand)


def solution(mesh):
    chips = mesh.devices.shape[0] // 2
    split = Mesh(
        mesh.devices.reshape(chips, 2, mesh.devices.shape[1]), ("tmc", "core", "panel")
    )
    in_specs = (P(TM, "panel"), P(TM, None), P(TM), P(), P(), P())
    out_specs = (P(TM, "panel"), P("panel"))
    return jax.shard_map(body, mesh=split, in_specs=in_specs, out_specs=out_specs, check_vma=False)
```
